256 devices in a mesh: seq: 64 (over y, x, z_lo), tp: 4 (over z_hi, core).
Axes of the slice: x: 4, y: 4, z: 8 (z_hi: 2, z_lo: 4; z = z_hi * 4 + z_lo), core: 2. Of those that a mesh axis runs over, the one named last changes fastest.
Arguments:
- queries: bfloat16 [8192, 4096], P('seq', 'tp'), may hold values from -6 to 6
- keys: bfloat16 [8192, 4096], P('seq', 'tp'), may hold values from -6 to 6
- values: bfloat16 [8192, 4096], P('seq', 'tp'), may hold values from -6 to 6
- w_out: bfloat16 [4096, 4096], P('seq', 'tp'), may hold values from -0.09375 to 0.09375
- taps: bfloat16 [4096, 128], P('tp'), may hold values from -0.6 to 0.6, as said below
- seg_ids: int32 [64], replicated, may hold values from 0 to 7, never falling along the last dimension, each value on 1 to 32 neighbouring positions
- cotangent: bfloat16 [8192, 4096], P('seq', 'tp'), may hold values from -6 to 6
Outputs:
- outputs: bfloat16 [8192, 4096], P('seq', 'tp')
- grad_queries: bfloat16 [8192, 4096], P('seq', 'tp')
- grad_keys: bfloat16 [8192, 4096], P('seq', 'tp')
- grad_values: bfloat16 [8192, 4096], P('seq', 'tp')
- taps_grad: float32 [4096, 128], P(('tp', 'seq'))
The draws below stay inside these ranges and needn't reach their ends.
Inputs may be any that keep to these rules, and one draw needn't show every extreme that they name: `seg_ids`: ids never fall along the pack, each segment covers 1 to 32 blocks. taps decay along the lag at a rate of each channel.
All inputs are finite; a program needn't handle non-finite values.
Results may differ from the reference program's by a relative error of at most 0.013.
Values may be sent and summed in bfloat16 or wider, within the bound.
A program may use at most 64 MiB of HBM per device.

```python
import math
import jax
import jax.numpy as jnp
import numpy as np
from jax import lax

C = 4096
D = 4096
FILT = 128
TOKENS = 8192
BLOCKS = 64
SEGS = 8
SEG_MOST = 32


def draw_taps(key, part):
    rate_key, amp_key = jax.random.split(jax.random.fold_in(key, 11))
    rates = jnp.exp(jax.random.uniform(rate_key, (C, 1), jnp.float32, math.log(0.004), math.log(0.08)))
    lags = jnp.arange(FILT, dtype=jnp.float32)[None, :]
    amps = jnp.clip(jax.random.normal(amp_key, (C, FILT), jnp.float32), -4.0, 4.0)
    return (0.15 * amps * jnp.exp(-rates * lags)).astype(jnp.bfloat16)


def block_levels(own_key, shape, pieces, smallest, high):
    def one(dim, blocks):
        heights = jax.random.uniform(jax.random.fold_in(jax.random.fold_in(own_key, 6), dim), (blocks,), jnp.float32, smallest / len(pieces), high / len(pieces))
        return jnp.repeat(jnp.exp(heights), shape[dim] // blocks).reshape((-1,) + (1,) * (len(shape) - dim - 1))

    gain = one(*pieces[0])
    for cut in pieces[1:]:
        gain = gain * one(*cut)
    return gain


def length_profile(amount, total, most, skew):
    portions = [(1 << 20) // math.isqrt(standing ** skew) + 1 for standing in range(2, amount + 1)]
    surplus, counts = total - most - (amount - 1), [1] * (amount - 1)
    while surplus > 0:
        candidates = [i for i in range(amount - 1) if counts[i] < most]
        pool, left = sum([portions[i] for i in candidates]), surplus
        for i in candidates:
            more = min(most - counts[i], max(1, left * portions[i] // pool), surplus)
            counts[i] = counts[i] + more
            surplus = surplus - more
    return np.array([most] + counts)


def ragged_sizes(stream_key, count, total, bound, skew):
    if count == 2:
        one = jax.random.randint(stream_key, (), max(1, total - bound), min(bound, total - 1) + 1)
        return jnp.stack([one, total - one])
    sizes = jnp.asarray(length_profile(count, total, bound, skew), jnp.int32)
    pairs = (count - 1) // 2
    giver, receiver = sizes[1:1 + 2 * pairs:2], sizes[2:2 + 2 * pairs:2]
    margin = jnp.minimum(giver - 1, bound - receiver)
    passed = jax.random.randint(jax.random.fold_in(stream_key, 1), (pairs,), 0, 1 << 20) % (margin + 1)
    sizes = sizes.at[1:1 + 2 * pairs:2].set(giver - passed).at[2:2 + 2 * pairs:2].set(receiver + passed)
    return sizes[jax.random.permutation(jax.random.fold_in(stream_key, 2), count)]


def scatter_about(stream_key, extent, scale, limit, shards=(), kind=jnp.bfloat16):
    gain = block_levels(stream_key, extent, shards, -0.22, 0.18) if shards else 1.0
    drawn = jax.random.normal(stream_key, extent, jnp.float32) * scale * gain
    return jnp.minimum(jnp.maximum(drawn, -limit), limit).astype(kind)


def setup_inputs(seed: int = 0) -> dict:
    seeds = jax.random.split(jax.random.key(seed), 8)
    return {
        "queries": scatter_about(seeds[0], (TOKENS, C), 1.0, 6.0, ((0, 64), (1, 4))),
        "keys": scatter_about(seeds[1], (TOKENS, C), 1.0, 6.0, ((0, 64), (1, 4))),
        "values": scatter_about(seeds[2], (TOKENS, C), 1.0, 6.0, ((0, 64), (1, 4))),
        "w_out": scatter_about(seeds[3], (C, D), C ** -0.5, 0.09375, ((0, 64), (1, 4))),
        "taps": draw_taps(jax.random.fold_in(seeds[7], 71), 0),
        "seg_ids": jnp.searchsorted(jnp.cumsum(ragged_sizes(seeds[5], SEGS, BLOCKS, SEG_MOST, 0)), jnp.arange(BLOCKS), side="right").astype(jnp.int32),
        "cotangent": scatter_about(seeds[6], (TOKENS, D), 1.0, 6.0, ((0, 64), (1, 4))),
    }


def lag_tables(length):
    rows = jnp.arange(length)[:, None]
    cols = jnp.arange(length)[None, :]
    lagged = (rows - cols).reshape(1, -1)
    shifts = jnp.arange(length)[:, None]
    inside = (lagged == shifts).astype(jnp.float32)
    across = (lagged + length == shifts).astype(jnp.float32)
    return inside, across


def dense_taps(taps_grp, table):
    count, length = taps_grp.shape
    dense = jnp.dot(taps_grp.astype(jnp.float32), table, precision=lax.Precision.HIGHEST)
    return dense.reshape(count, length, length)


def to_groups(blocks, group):
    count, length, chans = blocks.shape
    return blocks.reshape(count, length, chans // group, group).transpose(2, 0, 1, 3)


def from_groups(grouped):
    parts, count, length, group = grouped.shape
    return grouped.transpose(1, 2, 0, 3).reshape(count, length, parts * group)


def reference(queries, keys, values, w_out, taps, seg_ids, cotangent):
    tokens, chans = queries.shape
    length = taps.shape[1]
    count = tokens // length
    group = min(256, chans)
    inside, across = lag_tables(length)
    product = (keys.astype(jnp.float32) * values.astype(jnp.float32)).astype(jnp.bfloat16)
    linked = jnp.concatenate([jnp.zeros((1,), jnp.float32), (seg_ids[1:] == seg_ids[:-1]).astype(jnp.float32)])
    linked_next = jnp.concatenate([linked[1:], jnp.zeros((1,), jnp.float32)])
    blocks = product.reshape(count, length, chans)
    before = jnp.concatenate([jnp.zeros_like(blocks[:1]), blocks[:-1]], 0)
    taps_groups = taps.reshape(chans // group, group, length)

    def forward_group(items):
        taps_grp, current, prior = items
        near = dense_taps(taps_grp, inside)
        far = dense_taps(taps_grp, across)
        own = jnp.einsum("cij,bjc->bic", near, current.astype(jnp.float32), precision=lax.Precision.HIGHEST)
        back = jnp.einsum("cij,bjc->bic", far, prior.astype(jnp.float32), precision=lax.Precision.HIGHEST)
        return (own + linked[:, None, None] * back).astype(jnp.bfloat16)

    filtered_grp = lax.map(forward_group, (taps_groups, to_groups(blocks, group), to_groups(before, group)))
    filtered = from_groups(filtered_grp).reshape(tokens, chans)
    gated = (queries.astype(jnp.float32) * filtered.astype(jnp.float32)).astype(jnp.bfloat16)
    outputs = jnp.dot(gated, w_out, preferred_element_type=jnp.float32).astype(jnp.bfloat16)
    grad_gated = jnp.dot(cotangent, w_out.T, preferred_element_type=jnp.float32).astype(jnp.bfloat16)
    grad_filtered = (grad_gated.astype(jnp.float32) * queries.astype(jnp.float32)).astype(jnp.bfloat16)
    grad_queries = (grad_gated.astype(jnp.float32) * filtered.astype(jnp.float32)).astype(jnp.bfloat16)
    grads = grad_filtered.reshape(count, length, chans)
    after = jnp.concatenate([grads[1:], jnp.zeros_like(grads[:1])], 0)

    def backward_group(items):
        taps_grp, grad, later, current, prior = items
        near = dense_taps(taps_grp, inside)
        far = dense_taps(taps_grp, across)
        gradf = grad.astype(jnp.float32)
        own = jnp.einsum("cij,bic->bjc", near, gradf, precision=lax.Precision.HIGHEST)
        ahead = jnp.einsum("cij,bic->bjc", far, later.astype(jnp.float32), precision=lax.Precision.HIGHEST)
        back_grad = (own + linked_next[:, None, None] * ahead).astype(jnp.bfloat16)
        near_sum = jnp.einsum("bic,bjc->cij", gradf, current.astype(jnp.float32), precision=lax.Precision.HIGHEST)
        far_sum = jnp.einsum("bic,bjc->cij", gradf * linked[:, None, None], prior.astype(jnp.float32), precision=lax.Precision.HIGHEST)
        width = near_sum.shape[0]
        dims = (((1,), (1,)), ((), ()))
        taps_part = lax.dot_general(near_sum.reshape(width, -1), inside, dims, precision=lax.Precision.HIGHEST)
        taps_part = taps_part + lax.dot_general(far_sum.reshape(width, -1), across, dims, precision=lax.Precision.HIGHEST)
        return back_grad, taps_part

    back_grp, taps_grp_grad = lax.map(backward_group, (taps_groups, to_groups(grads, group), to_groups(after, group), to_groups(blocks, group), to_groups(before, group)))
    grad_product = from_groups(back_grp).reshape(tokens, chans).astype(jnp.float32)
    grad_keys = (grad_product * values.astype(jnp.float32)).astype(jnp.bfloat16)
    grad_values = (grad_product * keys.astype(jnp.float32)).astype(jnp.bfloat16)
    taps_grad = taps_grp_grad.reshape(chans, length)
    return (outputs, grad_queries, grad_keys, grad_values, taps_grad)
```

```python
import functools

import jax
import jax.numpy as jnp
import numpy as np
from jax import lax
from jax.experimental import pallas as pl
from jax.experimental.pallas import tpu as pltpu
from jax.sharding import Mesh
from jax.sharding import PartitionSpec as P

AXES = ("y", "x", "zl", "zh", "c")
SEQ = ("y", "x", "zl")
TP = ("zh", "c")
LEN = 128
MESH = pl.DeviceIdType.MESH
F32 = jnp.float32
BF16 = jnp.bfloat16


def split_hi_lo(mat):
    hi = np.asarray(mat, np.float32).astype(jnp.bfloat16)
    lo = (mat - hi.astype(np.float64)).astype(np.float32).astype(jnp.bfloat16)
    return np.stack([hi, lo])


def dft_tables():
    n = np.arange(LEN)
    ang = 2 * np.pi * np.outer(n, n) / (2 * LEN)
    alt = np.where(n % 2 == 0, 1.0, -1.0)
    fwd = np.concatenate([np.cos(ang), -np.sin(ang)], 0)
    fwd[LEN] = alt
    inv = np.concatenate([np.cos(ang), -np.sin(ang)], 1) / LEN
    inv[:, 0] = 0.5 / LEN
    inv[:, LEN] = alt * (0.5 / LEN)
    return split_hi_lo(fwd), split_hi_lo(inv)


def dot(a, b, dims=((1,), (0,))):
    return lax.dot_general(a, b, (dims, ((), ())), preferred_element_type=F32)


def kernel(
    q_ref, k_ref, v_ref, w_ref, taps_ref, seg_ref, cot_ref, fa_ref, ia_ref,
    out_ref, gq_ref, gk_ref, gv_ref, tg_ref,
    wbuf, prod, prev, tbuf, xbuf, fil, gbuf, ggs, ggr, gfb, gnx, gft,
    tgf, tgs, r1, s2, r2, s3, r3, ss, rs, ls,
):
    y, x, zl, zh, c = (lax.axis_index(a) for a in AXES)
    t = zh * 2 + c
    s = (y * 4 + x) * 4 + zl

    def shift(v, d):
        return lax.rem(v + (d % 4), 4)

    def zxor(j):
        lo, hi = lax.rem(zl, 2), zl // 2
        lo = 1 - lo if j & 1 else lo
        hi = 1 - hi if j & 2 else hi
        return hi * 2 + lo

    def at_x(d):
        return (y, shift(x, d), zl, zh, c)

    def at_y(d):
        return (shift(y, d), x, zl, zh, c)

    def at_z(j):
        return (y, x, zxor(j), zh, c)

    def at_s(d):
        p = lax.rem(s + (d % 64), 64)
        return (p // 16, lax.rem(p // 4, 4), lax.rem(p, 4), zh, c)

    sibling = (y, x, zl, zh, 1 - c)
    across = (y, x, zl, 1 - zh, c)
    diagonal = (y, x, zl, 1 - zh, 1 - c)

    barrier = pltpu.get_barrier_semaphore()
    partners = [across, diagonal, at_s(1), at_s(63), at_z(3), at_z(2), at_z(1), at_x(2), at_y(2)]
    partners += [at_x(1), at_x(3), at_y(1), at_y(3), sibling]
    for dev in partners:
        pl.semaphore_signal(barrier, inc=1, device_id=dev, device_id_type=MESH)

    keys_of = {}
    sends = []

    def make(key, src, dst, dev):
        i = keys_of.setdefault(key, len(keys_of))
        return pltpu.make_async_remote_copy(
            src_ref=src,
            dst_ref=dst,
            send_sem=ss.at[i],
            recv_sem=rs.at[i],
            device_id=dev,
            device_id_type=MESH,
        )

    def send(key, src, dst, dev):
        cp = make(key, src, dst, dev)
        cp.start()
        sends.append(cp)

    def recv(key, dst, dev):
        make(key, dst, dst, dev).wait_recv()

    own_w = pltpu.make_async_copy(
        w_ref, wbuf.at[pl.ds(pl.multiple_of(s * 64, 64), 64)], ls.at[0]
    )
    own_w.start()
    for i in range(4):
        cols = pl.ds(i * 256, 256)
        prod[:, cols] = (k_ref[:, cols].astype(F32) * v_ref[:, cols].astype(F32)).astype(BF16)

    def chunk(j, a, b, part=None):
        dx, dy = (a, b) if j % 2 == 0 else (b, a)
        off = ((shift(y, dy) * 4 + shift(x, dx)) * 4 + zxor(j)) * 64
        size = 64
        if part is not None:
            off, size = off + 32 * part, 32
        return wbuf.at[pl.ds(pl.multiple_of(off, size), size)]

    def step(j, first, d):
        along_x = (j % 2 == 0) == first
        return at_x(d) if along_x else at_y(d)

    def source(j, a):
        return w_ref if j == 0 and a == 0 else chunk(j, a, 0)

    def second(j, a):
        src = source(j, a)
        send(("u1", j, a), src, chunk(j, a, 0), step(j, False, 1))
        send(("u2", j, a), src, chunk(j, a, 0), step(j, False, -1))

    def s1(j):
        src = source(j, 0)
        send(("t1", j), src, chunk(j, 0, 0), step(j, True, 1))
        send(("t2", j), src, chunk(j, 0, 0), step(j, True, -1))
        second(j, 0)

    def s2_(j):
        recv(("t1", j), chunk(j, -1, 0), step(j, True, 1))
        send(("t3", j), chunk(j, -1, 0, 0), chunk(j, -1, 0, 0), step(j, True, 1))
        recv(("t2", j), chunk(j, 1, 0), step(j, True, -1))
        send(("t4", j), chunk(j, 1, 0, 1), chunk(j, 1, 0, 1), step(j, True, -1))
        second(j, -1)
        second(j, 1)

    def s3_(j):
        recv(("t3", j), chunk(j, 2, 0, 0), step(j, True, 1))
        recv(("t4", j), chunk(j, 2, 0, 1), step(j, True, -1))
        second(j, 2)

    def relay(j, a):
        recv(("u1", j, a), chunk(j, a, -1), step(j, False, 1))
        send(("u3", j, a), chunk(j, a, -1, 0), chunk(j, a, -1, 0), step(j, False, 1))
        recv(("u2", j, a), chunk(j, a, 1), step(j, False, -1))
        send(("u4", j, a), chunk(j, a, 1, 1), chunk(j, a, 1, 1), step(j, False, -1))

    def last(j, a):
        recv(("u3", j, a), chunk(j, a, 2, 0), step(j, False, 1))
        recv(("u4", j, a), chunk(j, a, 2, 1), step(j, False, -1))

    def own_place(j):
        return wbuf.at[pl.ds(pl.multiple_of(((y * 4 + x) * 4 + zxor(j)) * 64, 64), 64)]

    def half_of(p):
        return zl // 2 if p == 0 else 1 - zl // 2

    def gg_copy(p, dy):
        yy, h = shift(y, dy), half_of(p)
        delta = lax.rem(yy + 4 - t, 4)
        i = gg_base + p * 4 + delta
        return delta, pltpu.make_async_remote_copy(
            src_ref=ggs.at[yy, h],
            dst_ref=ggr.at[delta, h],
            send_sem=ss.at[i],
            recv_sem=rs.at[i],
            device_id=(y, x, zl, yy // 2, lax.rem(yy, 2)),
            device_id_type=MESH,
        )

    def batch(p, dy):
        yy, h = shift(y, dy), half_of(p)

        def one(i, carry):
            rows = pl.ds(pl.multiple_of(yy * 1024 + i * 256 + h * 128, 128), 128)
            part = dot(cot_ref[...], wbuf[rows, :], ((1,), (1,)))
            ggs[yy, h, i] = part.astype(BF16)
            return carry

        lax.fori_loop(0, 4, one, 0)
        delta, cp = gg_copy(p, dy)

        @pl.when(delta != 0)
        def _():
            cp.start()

    gg_base = 160

    row = lax.broadcasted_iota(jnp.int32, (2 * LEN, 128), 0)
    sign = (1 - 2 * lax.rem(row, 2)).astype(F32)
    inner = lax.broadcasted_iota(jnp.int32, (LEN, 128), 0) != 0

    def dft(val):
        return dot(fa_ref[0], val) + dot(fa_ref[1], val)

    def idft(val):
        hi = val.astype(BF16)
        lo = (val - hi.astype(F32)).astype(BF16)
        return dot(ia_ref[0], hi) + dot(ia_ref[0], lo) + dot(ia_ref[1], hi)

    def cmul(a, b, conj):
        ar, ai, br, bi = a[:LEN], a[LEN:], b[:LEN], b[LEN:]
        ii = ai * bi
        if conj:
            re = ar * br + jnp.where(inner, ii, 0.0)
            im = jnp.where(inner, ai * br - ar * bi, ii)
        else:
            re = ar * br - jnp.where(inner, ii, 0.0)
            im = jnp.where(inner, ai * br + ar * bi, ii)
        return jnp.concatenate([re, im], 0)

    def strips(fn):
        def one(e, carry):
            fn(e, pl.ds(pl.multiple_of(e * 128, 128), 128))
            return carry

        lax.fori_loop(0, 8, one, 0)

    here = seg_ref[s]
    back = seg_ref[jnp.maximum(s - 1, 0)]
    ahead = seg_ref[jnp.minimum(s + 1, 63)]
    linked = jnp.where(jnp.logical_and(s > 0, here == back), 1.0, 0.0).astype(F32)
    linked_next = jnp.where(jnp.logical_and(s < 63, here == ahead), 1.0, 0.0).astype(F32)

    pl.semaphore_wait(barrier, len(partners))

    s1(0)
    send("z1", w_ref, own_place(0), at_z(1))
    send("z2", w_ref, own_place(0), at_z(2))
    send("halo", prod, prev, at_s(1))

    def spectra(e, cols):
        tap = taps_ref[cols, :]
        tbuf[e] = dot(fa_ref[0], tap, ((1,), (1,))) + dot(fa_ref[1], tap, ((1,), (1,)))
        xbuf[e] = dft(prod[:, cols])

    strips(spectra)
    own_w.wait()

    recv("z1", own_place(1), at_z(1))
    send("z3", own_place(1), own_place(1), at_z(2))
    s1(1)
    s2_(0)
    s2_(1)
    s3_(0)
    s3_(1)
    relay(0, 0)
    relay(1, 0)
    recv("z2", own_place(2), at_z(2))
    s1(2)
    recv("halo", prev, at_s(1))

    def forward(e, cols):
        spec = xbuf[e] + linked * (sign * dft(prev[:, cols]))
        xbuf[e] = spec
        filt = idft(cmul(spec, tbuf[e], False)).astype(BF16)
        fil[:, cols] = filt
        gbuf[t, :, cols] = (q_ref[:, cols].astype(F32) * filt.astype(F32)).astype(BF16)

    strips(forward)
    t_sib, t_acr, t_dia = zh * 2 + 1 - c, (1 - zh) * 2 + c, (1 - zh) * 2 + 1 - c
    send("g2", gbuf.at[t], gbuf.at[t], across)
    send("g1", gbuf.at[t], gbuf.at[t], sibling)

    relay(0, -1)
    relay(1, -1)
    relay(0, 1)
    relay(1, 1)
    recv("z3", own_place(3), at_z(2))
    s1(3)
    s2_(2)
    relay(0, 2)
    relay(1, 2)
    s2_(3)
    last(0, 0)
    last(1, 0)
    batch(0, 0)
    s3_(2)
    s3_(3)
    relay(2, 0)
    relay(3, 0)
    for a in (-1, 1):
        last(0, a)
        last(1, a)
    last(0, 2)
    batch(0, -1)
    relay(2, -1)
    relay(3, -1)
    batch(0, 1)
    relay(2, 1)
    relay(3, 1)
    last(1, 2)
    batch(0, 2)
    relay(2, 2)
    relay(3, 2)
    recv("g2", gbuf.at[t_acr], across)
    send("g3", gbuf.at[t_acr], gbuf.at[t_acr], sibling)
    last(2, 0)
    last(3, 0)
    batch(1, 0)
    for a in (-1, 1):
        last(2, a)
        last(3, a)
    last(2, 2)
    batch(1, -1)
    batch(1, 1)
    last(3, 2)
    batch(1, 2)

    for p in range(2):
        for delta in range(1, 4):
            h = half_of(p)
            i = gg_base + p * 4 + delta
            pltpu.make_async_remote_copy(
                src_ref=ggr.at[delta, h],
                dst_ref=ggr.at[delta, h],
                send_sem=ss.at[i],
                recv_sem=rs.at[i],
                device_id=sibling,
                device_id_type=MESH,
            ).wait_recv()

    def gradients(e, cols):
        h, i = lax.rem(e, 2), e // 2
        total = ggs[t, h, i].astype(F32)
        for delta in range(1, 4):
            total = total + ggr[delta, h, i].astype(F32)
        gg = total.astype(BF16).astype(F32)
        gfb[:, cols] = (gg * q_ref[:, cols].astype(F32)).astype(BF16)
        gq_ref[:, cols] = (gg * fil[:, cols].astype(F32)).astype(BF16)

    strips(gradients)
    send("ghalo", gfb, gnx, at_s(-1))

    def taps_part(e, cols):
        spec = dft(gfb[:, cols])
        gft[e] = spec
        part = idft(cmul(spec, xbuf[e], True)).T
        tgf[cols, :] = part
        tgs[cols, :] = part.astype(BF16)

    strips(taps_part)

    def rows_of(place, size):
        return pl.ds(pl.multiple_of(place * size, size), size)

    for d in range(1, 4):
        send(("r1", d), tgs.at[rows_of(shift(y, d), 256)], r1.at[d - 1], at_y(d))

    recv("g1", gbuf.at[t_sib], sibling)
    recv("g3", gbuf.at[t_dia], sibling)

    def outputs(n):
        cols = pl.ds(n * 256, 256)
        total = dot(gbuf[0], wbuf[0:1024, cols])
        for i in range(1, 4):
            total = total + dot(gbuf[i], wbuf[i * 1024 : (i + 1) * 1024, cols])
        out_ref[:, cols] = total.astype(BF16)

    outputs(0)
    outputs(1)
    for d in range(1, 4):
        recv(("r1", d), r1.at[d - 1], at_y(d))
    total = tgf[rows_of(y, 256), :]
    for d in range(3):
        total = total + r1[d].astype(F32)
    s2[...] = total
    for d in range(1, 4):
        send(("r2", d), s2.at[rows_of(shift(x, d), 64)], r2.at[d - 1], at_x(d))
    outputs(2)
    for d in range(1, 4):
        recv(("r2", d), r2.at[d - 1], at_x(d))
    total = s2[rows_of(x, 64), :]
    for d in range(3):
        total = total + r2[d]
    s3[...] = total
    for d in range(1, 4):
        send(("r3", d), s3.at[rows_of(zxor(d), 16)], r3.at[d - 1], at_z(d))
    outputs(3)
    recv("ghalo", gnx, at_s(-1))

    def backward(e, cols):
        spec = gft[e] + linked_next * (sign * dft(gnx[:, cols]))
        gp = idft(cmul(spec, tbuf[e], True)).astype(BF16).astype(F32)
        gk_ref[:, cols] = (gp * v_ref[:, cols].astype(F32)).astype(BF16)
        gv_ref[:, cols] = (gp * k_ref[:, cols].astype(F32)).astype(BF16)

    strips(backward)
    for d in range(1, 4):
        recv(("r3", d), r3.at[d - 1], at_z(d))
    total = s3[rows_of(zl, 16), :]
    for d in range(3):
        total = total + r3[d]
    tg_ref[...] = total

    for cp in sends:
        cp.wait_send()
    for p in range(2):
        for dy in (0, -1, 1, 2):
            delta, cp = gg_copy(p, dy)

            @pl.when(delta != 0)
            def _(cp=cp):
                cp.wait_send()

    assert len(keys_of) <= gg_base


def on_device(queries, keys, values, w_out, taps, seg_ids, cotangent):
    fwd, inv = dft_tables()
    block = queries.shape
    vmem = pl.BlockSpec(memory_space=pltpu.VMEM)
    smem = pl.BlockSpec(memory_space=pltpu.SMEM)
    outs = [jax.ShapeDtypeStruct(block, BF16)] * 4 + [jax.ShapeDtypeStruct((16, LEN), F32)]
    scratch = [
        pltpu.VMEM((4096, 1024), BF16),
        pltpu.VMEM(block, BF16),
        pltpu.VMEM(block, BF16),
        pltpu.VMEM((8, 256, 128), F32),
        pltpu.VMEM((8, 256, 128), F32),
        pltpu.VMEM(block, BF16),
        pltpu.VMEM((4, *block), BF16),
        pltpu.VMEM((4, 2, 4, 128, 128), BF16),
        pltpu.VMEM((4, 2, 4, 128, 128), BF16),
        pltpu.VMEM(block, BF16),
        pltpu.VMEM(block, BF16),
        pltpu.VMEM((8, 256, 128), F32),
        pltpu.VMEM((1024, LEN), F32),
        pltpu.VMEM((1024, LEN), BF16),
        pltpu.VMEM((3, 256, LEN), BF16),
        pltpu.VMEM((256, LEN), F32),
        pltpu.VMEM((3, 64, LEN), F32),
        pltpu.VMEM((64, LEN), F32),
        pltpu.VMEM((3, 16, LEN), F32),
        pltpu.SemaphoreType.DMA((168,)),
        pltpu.SemaphoreType.DMA((168,)),
        pltpu.SemaphoreType.DMA((1,)),
    ]
    return pl.pallas_call(
        kernel,
        out_shape=outs,
        in_specs=[vmem] * 5 + [smem] + [vmem] * 3,
        out_specs=[vmem] * 5,
        scratch_shapes=scratch,
        compiler_params=pltpu.CompilerParams(
            collective_id=0, has_side_effects=True, vmem_limit_bytes=44 * 1024 * 1024
        ),
        name="hyena",
    )(queries, keys, values, w_out, taps, seg_ids, cotangent, jnp.asarray(fwd), jnp.asarray(inv))


def solution(mesh):
    split = Mesh(mesh.devices.reshape(4, 4, 4, 2, 2), AXES)
    rows = P(SEQ, TP)
    in_specs = (rows, rows, rows, rows, P(TP, None), P(), rows)
    out_specs = (rows, rows, rows, rows, P(TP + SEQ, None))
    return jax.shard_map(
        on_device, mesh=split, in_specs=in_specs, out_specs=out_specs, check_vma=False
    )
```

```python
import functools

import jax
import jax.numpy as jnp
import numpy as np
from jax import lax
from jax.experimental import pallas as pl
from jax.experimental.pallas import tpu as pltpu
from jax.sharding import Mesh
from jax.sharding import PartitionSpec as P

AXES = ("y", "x", "zl", "zh", "c")
SEQ = ("y", "x", "zl")
TP = ("zh", "c")
LEN = 128
MESH = pl.DeviceIdType.MESH
F32 = jnp.float32
BF16 = jnp.bfloat16


def split_hi_lo(mat):
    hi = np.asarray(mat, np.float32).astype(jnp.bfloat16)
    lo = (mat - hi.astype(np.float64)).astype(np.float32).astype(jnp.bfloat16)
    return np.stack([hi, lo])


def dft_tables():
    n = np.arange(LEN)
    ang = 2 * np.pi * np.outer(n, n) / (2 * LEN)
    alt = np.where(n % 2 == 0, 1.0, -1.0)
    fwd = np.concatenate([np.cos(ang), -np.sin(ang)], 0)
    fwd[LEN] = alt
    inv = np.concatenate([np.cos(ang), -np.sin(ang)], 1) / LEN
    inv[:, 0] = 0.5 / LEN
    inv[:, LEN] = alt * (0.5 / LEN)
    return split_hi_lo(fwd), split_hi_lo(inv)


def dot(a, b, dims=((1,), (0,))):
    return lax.dot_general(a, b, (dims, ((), ())), preferred_element_type=F32)


def kernel(
    q_hbm, k_hbm, v_hbm, w_hbm, taps_hbm, seg_ref, cot_hbm, fa_hbm, ia_hbm,
    out_ref, gq_ref, gk_ref, gv_ref, tg_ref,
    q_ref, k_ref, v_ref, w_ref, taps_ref, cot_ref, fa_ref, ia_ref,
    wbuf, prod, prev, tbuf, xbuf, fil, gbuf, ggs, ggr, gfb, gnx, gft,
    tgf, tgs, r1, s2, r2, s3, r3, ss, rs, ls,
):
    y, x, zl, zh, c = (lax.axis_index(a) for a in AXES)
    t = zh * 2 + c
    s = (y * 4 + x) * 4 + zl

    loads = []
    pairs = [(w_hbm, w_ref), (k_hbm, k_ref), (v_hbm, v_ref), (taps_hbm, taps_ref)]
    pairs += [(fa_hbm, fa_ref), (ia_hbm, ia_ref), (q_hbm, q_ref), (cot_hbm, cot_ref)]
    for i, (src, dst) in enumerate(pairs):
        cp = pltpu.make_async_copy(src, dst, ls.at[1 + i])
        cp.start()
        loads.append(cp)

    def shift(v, d):
        return lax.rem(v + (d % 4), 4)

    def zxor(j):
        lo, hi = lax.rem(zl, 2), zl // 2
        lo = 1 - lo if j & 1 else lo
        hi = 1 - hi if j & 2 else hi
        return hi * 2 + lo

    def at_x(d):
        return (y, shift(x, d), zl, zh, c)

    def at_y(d):
        return (shift(y, d), x, zl, zh, c)

    def at_z(j):
        return (y, x, zxor(j), zh, c)

    def at_s(d):
        p = lax.rem(s + (d % 64), 64)
        return (p // 16, lax.rem(p // 4, 4), lax.rem(p, 4), zh, c)

    sibling = (y, x, zl, zh, 1 - c)
    across = (y, x, zl, 1 - zh, c)
    diagonal = (y, x, zl, 1 - zh, 1 - c)

    barrier = pltpu.get_barrier_semaphore()
    partners = [across, diagonal, at_s(1), at_s(63), at_z(3), at_z(2), at_z(1), at_x(2), at_y(2)]
    partners += [at_x(1), at_x(3), at_y(1), at_y(3), sibling]
    for dev in partners:
        pl.semaphore_signal(barrier, inc=1, device_id=dev, device_id_type=MESH)

    keys_of = {}
    sends = []

    def make(key, src, dst, dev):
        i = keys_of.setdefault(key, len(keys_of))
        return pltpu.make_async_remote_copy(
            src_ref=src,
            dst_ref=dst,
            send_sem=ss.at[i],
            recv_sem=rs.at[i],
            device_id=dev,
            device_id_type=MESH,
        )

    def send(key, src, dst, dev):
        cp = make(key, src, dst, dev)
        cp.start()
        sends.append(cp)

    def recv(key, dst, dev):
        make(key, dst, dst, dev).wait_recv()

    for cp in loads[:3]:
        cp.wait()
    own_w = pltpu.make_async_copy(
        w_ref, wbuf.at[pl.ds(pl.multiple_of(s * 64, 64), 64)], ls.at[0]
    )
    own_w.start()
    for i in range(4):
        cols = pl.ds(i * 256, 256)
        prod[:, cols] = (k_ref[:, cols].astype(F32) * v_ref[:, cols].astype(F32)).astype(BF16)

    def chunk(j, a, b, part=None):
        dx, dy = (a, b) if j % 2 == 0 else (b, a)
        off = ((shift(y, dy) * 4 + shift(x, dx)) * 4 + zxor(j)) * 64
        size = 64
        if part is not None:
            off, size = off + 32 * part, 32
        return wbuf.at[pl.ds(pl.multiple_of(off, size), size)]

    def step(j, first, d):
        along_x = (j % 2 == 0) == first
        return at_x(d) if along_x else at_y(d)

    def source(j, a):
        return w_ref if j == 0 and a == 0 else chunk(j, a, 0)

    def second(j, a):
        src = source(j, a)
        send(("u1", j, a), src, chunk(j, a, 0), step(j, False, 1))
        send(("u2", j, a), src, chunk(j, a, 0), step(j, False, -1))

    def s1(j):
        src = source(j, 0)
        send(("t1", j), src, chunk(j, 0, 0), step(j, True, 1))
        send(("t2", j), src, chunk(j, 0, 0), step(j, True, -1))
        second(j, 0)

    def s2_(j):
        recv(("t1", j), chunk(j, -1, 0), step(j, True, 1))
        send(("t3", j), chunk(j, -1, 0, 0), chunk(j, -1, 0, 0), step(j, True, 1))
        recv(("t2", j), chunk(j, 1, 0), step(j, True, -1))
        send(("t4", j), chunk(j, 1, 0, 1), chunk(j, 1, 0, 1), step(j, True, -1))
        second(j, -1)
        second(j, 1)

    def s3_(j):
        recv(("t3", j), chunk(j, 2, 0, 0), step(j, True, 1))
        recv(("t4", j), chunk(j, 2, 0, 1), step(j, True, -1))
        second(j, 2)

    def relay(j, a):
        recv(("u1", j, a), chunk(j, a, -1), step(j, False, 1))
        send(("u3", j, a), chunk(j, a, -1, 0), chunk(j, a, -1, 0), step(j, False, 1))
        recv(("u2", j, a), chunk(j, a, 1), step(j, False, -1))
        send(("u4", j, a), chunk(j, a, 1, 1), chunk(j, a, 1, 1), step(j, False, -1))

    def last(j, a):
        recv(("u3", j, a), chunk(j, a, 2, 0), step(j, False, 1))
        recv(("u4", j, a), chunk(j, a, 2, 1), step(j, False, -1))

    def own_place(j):
        return wbuf.at[pl.ds(pl.multiple_of(((y * 4 + x) * 4 + zxor(j)) * 64, 64), 64)]

    def half_of(p):
        return zl // 2 if p == 0 else 1 - zl // 2

    def gg_copy(p, dy):
        yy, h = shift(y, dy), half_of(p)
        delta = lax.rem(yy + 4 - t, 4)
        i = gg_base + p * 4 + delta
        return delta, pltpu.make_async_remote_copy(
            src_ref=ggs.at[yy, h],
            dst_ref=ggr.at[delta, h],
            send_sem=ss.at[i],
            recv_sem=rs.at[i],
            device_id=(y, x, zl, yy // 2, lax.rem(yy, 2)),
            device_id_type=MESH,
        )

    def batch(p, dy):
        yy, h = shift(y, dy), half_of(p)

        def one(i, carry):
            rows = pl.ds(pl.multiple_of(yy * 1024 + i * 256 + h * 128, 128), 128)
            part = dot(cot_ref[...], wbuf[rows, :], ((1,), (1,)))
            ggs[yy, h, i] = part.astype(BF16)
            return carry

        lax.fori_loop(0, 4, one, 0)
        delta, cp = gg_copy(p, dy)

        @pl.when(delta != 0)
        def _():
            cp.start()

    gg_base = 160
    halo_base = 168

    row = lax.broadcasted_iota(jnp.int32, (2 * LEN, 128), 0)
    sign = (1 - 2 * lax.rem(row, 2)).astype(F32)
    inner = lax.broadcasted_iota(jnp.int32, (LEN, 128), 0) != 0

    def dft(val):
        return dot(fa_ref[0], val) + dot(fa_ref[1], val)

    def idft(val):
        hi = val.astype(BF16)
        lo = (val - hi.astype(F32)).astype(BF16)
        return dot(ia_ref[0], hi) + dot(ia_ref[0], lo) + dot(ia_ref[1], hi)

    def cmul(a, b, conj):
        ar, ai, br, bi = a[:LEN], a[LEN:], b[:LEN], b[LEN:]
        ii = ai * bi
        if conj:
            re = ar * br + jnp.where(inner, ii, 0.0)
            im = jnp.where(inner, ai * br - ar * bi, ii)
        else:
            re = ar * br - jnp.where(inner, ii, 0.0)
            im = jnp.where(inner, ai * br + ar * bi, ii)
        return jnp.concatenate([re, im], 0)

    def strips(fn, first=0, after=8):
        def one(e, carry):
            fn(e, pl.ds(pl.multiple_of(e * 128, 128), 128))
            return carry

        lax.fori_loop(first, after, one, 0)

    here = seg_ref[s]
    back = seg_ref[jnp.maximum(s - 1, 0)]
    ahead = seg_ref[jnp.minimum(s + 1, 63)]
    linked = jnp.where(jnp.logical_and(s > 0, here == back), 1.0, 0.0).astype(F32)
    linked_next = jnp.where(jnp.logical_and(s < 63, here == ahead), 1.0, 0.0).astype(F32)

    for cp in loads[3:]:
        cp.wait()
    pl.semaphore_wait(barrier, len(partners))

    s1(0)
    send("z1", w_ref, own_place(0), at_z(1))
    send("z2", w_ref, own_place(0), at_z(2))
    send("halo", prod, prev, at_s(1))

    def spectra(e, cols):
        tap = taps_ref[cols, :]
        tbuf[e] = dot(fa_ref[0], tap, ((1,), (1,))) + dot(fa_ref[1], tap, ((1,), (1,)))
        xbuf[e] = dft(prod[:, cols])

    strips(spectra)
    own_w.wait()

    recv("z1", own_place(1), at_z(1))
    send("z3", own_place(1), own_place(1), at_z(2))
    s1(1)
    s2_(0)
    s2_(1)
    s3_(0)
    s3_(1)
    relay(0, 0)
    relay(1, 0)
    recv("z2", own_place(2), at_z(2))
    s1(2)
    recv("halo", prev, at_s(1))

    def forward(e, cols):
        spec = xbuf[e] + linked * (sign * dft(prev[:, cols]))
        xbuf[e] = spec
        filt = idft(cmul(spec, tbuf[e], False)).astype(BF16)
        fil[:, cols] = filt
        gbuf[t, :, cols] = (q_ref[:, cols].astype(F32) * filt.astype(F32)).astype(BF16)

    strips(forward)
    t_sib, t_acr, t_dia = zh * 2 + 1 - c, (1 - zh) * 2 + c, (1 - zh) * 2 + 1 - c
    send("g2", gbuf.at[t], gbuf.at[t], across)
    send("g1", gbuf.at[t], gbuf.at[t], sibling)

    relay(0, -1)
    relay(1, -1)
    relay(0, 1)
    relay(1, 1)
    recv("z3", own_place(3), at_z(2))
    s1(3)
    s2_(2)
    relay(0, 2)
    relay(1, 2)
    s2_(3)
    last(0, 0)
    last(1, 0)
    batch(0, 0)
    s3_(2)
    s3_(3)
    relay(2, 0)
    relay(3, 0)
    for a in (-1, 1):
        last(0, a)
        last(1, a)
    last(0, 2)
    batch(0, -1)
    relay(2, -1)
    relay(3, -1)
    batch(0, 1)
    relay(2, 1)
    relay(3, 1)
    last(1, 2)
    batch(0, 2)
    relay(2, 2)
    relay(3, 2)
    recv("g2", gbuf.at[t_acr], across)
    send("g3", gbuf.at[t_acr], gbuf.at[t_acr], sibling)
    last(2, 0)
    last(3, 0)
    batch(1, 0)
    for a in (-1, 1):
        last(2, a)
        last(3, a)
    last(2, 2)
    batch(1, -1)
    batch(1, 1)
    last(3, 2)
    batch(1, 2)

    def rows_of(place, size):
        return pl.ds(pl.multiple_of(place * size, size), size)

    def half_copy(base, h, src, dst, dev):
        return pltpu.make_async_remote_copy(
            src_ref=src,
            dst_ref=dst,
            send_sem=ss.at[base + h],
            recv_sem=rs.at[base + h],
            device_id=dev,
            device_id_type=MESH,
        )

    def half_tail(p):
        h = half_of(p)
        for delta in range(1, 4):
            i = gg_base + p * 4 + delta
            pltpu.make_async_remote_copy(
                src_ref=ggr.at[delta, h],
                dst_ref=ggr.at[delta, h],
                send_sem=ss.at[i],
                recv_sem=rs.at[i],
                device_id=sibling,
                device_id_type=MESH,
            ).wait_recv()

        def cols_of(i):
            return pl.ds(pl.multiple_of(i * 256 + h * 128, 128), 128)

        def gradients(i, carry):
            cols = cols_of(i)
            total = ggs[t, h, i].astype(F32)
            for delta in range(1, 4):
                total = total + ggr[delta, h, i].astype(F32)
            gg = total.astype(BF16).astype(F32)
            gfb[h, i] = (gg * q_ref[:, cols].astype(F32)).astype(BF16)
            gq_ref[:, cols] = (gg * fil[:, cols].astype(F32)).astype(BF16)
            return carry

        lax.fori_loop(0, 4, gradients, 0)
        half_copy(halo_base, h, gfb.at[h], gnx.at[h], at_s(-1)).start()

        def taps_part(i, carry):
            cols = cols_of(i)
            spec = dft(gfb[h, i])
            e = i * 2 + h
            gft[e] = spec
            part = idft(cmul(spec, xbuf[e], True)).T
            tgf[cols, :] = part
            tgs[cols, :] = part.astype(BF16)
            return carry

        lax.fori_loop(0, 4, taps_part, 0)
        for d in (2, 1, 3):
            rows = pl.ds(pl.multiple_of(shift(y, d) * 256 + h * 128, 128), 128)
            here = pl.ds(pl.multiple_of(h * 128, 128), 128)
            send(("r1", p, d), tgs.at[rows], r1.at[d - 1, here], at_y(d))

    def r1_rows(p):
        return pl.ds(pl.multiple_of(half_of(p) * 128, 128), 128)

    half_tail(0)
    recv("g1", gbuf.at[t_sib], sibling)
    recv("g3", gbuf.at[t_dia], sibling)

    def outputs(n):
        cols = pl.ds(n * 256, 256)
        total = dot(gbuf[0], wbuf[0:1024, cols])
        for i in range(1, 4):
            total = total + dot(gbuf[i], wbuf[i * 1024 : (i + 1) * 1024, cols])
        out_ref[:, cols] = total.astype(BF16)

    outputs(0)
    outputs(1)
    outputs(2)
    half_tail(1)
    outputs(3)
    for p in range(2):
        for d in range(1, 4):
            recv(("r1", p, d), r1.at[d - 1, r1_rows(p)], at_y(d))
    total = tgf[rows_of(y, 256), :]
    for d in range(3):
        total = total + r1[d].astype(F32)
    s2[...] = total
    for d in (2, 1, 3):
        send(("r2", d), s2.at[rows_of(shift(x, d), 64)], r2.at[d - 1], at_x(d))

    def backward(e, cols):
        spec = gft[e] + linked_next * (sign * dft(gnx[lax.rem(e, 2), e // 2]))
        gp = idft(cmul(spec, tbuf[e], True)).astype(BF16).astype(F32)
        gk_ref[:, cols] = (gp * v_ref[:, cols].astype(F32)).astype(BF16)
        gv_ref[:, cols] = (gp * k_ref[:, cols].astype(F32)).astype(BF16)

    for h in range(2):
        half_copy(halo_base, h, gfb.at[h], gnx.at[h], at_s(-1)).wait_recv()
    strips(backward, 0, 4)
    for d in range(1, 4):
        recv(("r2", d), r2.at[d - 1], at_x(d))
    total = s2[rows_of(x, 64), :]
    for d in range(3):
        total = total + r2[d]
    s3[...] = total
    for d in (3, 2, 1):
        send(("r3", d), s3.at[rows_of(zxor(d), 16)], r3.at[d - 1], at_z(d))
    strips(backward, 4, 8)
    for d in range(1, 4):
        recv(("r3", d), r3.at[d - 1], at_z(d))
    total = s3[rows_of(zl, 16), :]
    for d in range(3):
        total = total + r3[d]
    tg_ref[...] = total

    for h in range(2):
        half_copy(halo_base, h, gfb.at[h], gnx.at[h], at_s(-1)).wait_send()
    for cp in sends:
        cp.wait_send()
    for p in range(2):
        for dy in (0, -1, 1, 2):
            delta, cp = gg_copy(p, dy)

            @pl.when(delta != 0)
            def _(cp=cp):
                cp.wait_send()

    assert len(keys_of) <= gg_base


def write_out(*refs):
    ins, outs, bufs, sem = refs[:5], refs[5:10], refs[10:15], refs[15]
    reads = [pltpu.make_async_copy(ins[i], bufs[i], sem.at[i]) for i in range(5)]
    writes = [pltpu.make_async_copy(bufs[i], outs[i], sem.at[5 + i]) for i in range(5)]
    for cp in reads:
        cp.start()
    for read, write in zip(reads, writes):
        read.wait()
        write.start()
    for cp in writes:
        cp.wait()


def on_device(queries, keys, values, w_out, taps, seg_ids, cotangent):
    fwd, inv = dft_tables()
    block = queries.shape
    vmem = pl.BlockSpec(memory_space=pltpu.VMEM)
    hbm = pl.BlockSpec(memory_space=pl.ANY)
    smem = pl.BlockSpec(memory_space=pltpu.SMEM)
    outs = [jax.ShapeDtypeStruct(block, BF16)] * 4 + [jax.ShapeDtypeStruct((16, LEN), F32)]
    scratch = [
        pltpu.VMEM(block, BF16),
        pltpu.VMEM(block, BF16),
        pltpu.VMEM(block, BF16),
        pltpu.VMEM((64, 1024), BF16),
        pltpu.VMEM((1024, LEN), BF16),
        pltpu.VMEM(block, BF16),
        pltpu.VMEM((2, 256, 128), BF16),
        pltpu.VMEM((2, 128, 256), BF16),
        pltpu.VMEM((4096, 1024), BF16),
        pltpu.VMEM(block, BF16),
        pltpu.VMEM(block, BF16),
        pltpu.VMEM((8, 256, 128), F32),
        pltpu.VMEM((8, 256, 128), F32),
        pltpu.VMEM(block, BF16),
        pltpu.VMEM((4, *block), BF16),
        pltpu.VMEM((4, 2, 4, 128, 128), BF16),
        pltpu.VMEM((4, 2, 4, 128, 128), BF16),
        pltpu.VMEM((2, 4, 128, 128), BF16),
        pltpu.VMEM((2, 4, 128, 128), BF16),
        pltpu.VMEM((8, 256, 128), F32),
        pltpu.VMEM((1024, LEN), F32),
        pltpu.VMEM((1024, LEN), BF16),
        pltpu.VMEM((3, 256, LEN), BF16),
        pltpu.VMEM((256, LEN), F32),
        pltpu.VMEM((3, 64, LEN), F32),
        pltpu.VMEM((64, LEN), F32),
        pltpu.VMEM((3, 16, LEN), F32),
        pltpu.SemaphoreType.DMA((170,)),
        pltpu.SemaphoreType.DMA((170,)),
        pltpu.SemaphoreType.DMA((9,)),
    ]
    results = pl.pallas_call(
        kernel,
        out_shape=outs,
        in_specs=[hbm] * 5 + [smem] + [hbm] * 3,
        out_specs=[vmem] * 5,
        scratch_shapes=scratch,
        compiler_params=pltpu.CompilerParams(
            collective_id=0, has_side_effects=True, vmem_limit_bytes=67043328
        ),
        name="hyena",
    )(queries, keys, values, w_out, taps, seg_ids, cotangent, jnp.asarray(fwd), jnp.asarray(inv))
    return pl.pallas_call(
        write_out,
        out_shape=outs,
        in_specs=[hbm] * 5,
        out_specs=[hbm] * 5,
        scratch_shapes=[pltpu.VMEM(o.shape, o.dtype) for o in outs]
        + [pltpu.SemaphoreType.DMA((10,))],
        compiler_params=pltpu.CompilerParams(vmem_limit_bytes=67043328),
        name="write_out",
    )(*results)


def solution(mesh):
    split = Mesh(mesh.devices.reshape(4, 4, 4, 2, 2), AXES)
    rows = P(SEQ, TP)
    in_specs = (rows, rows, rows, rows, P(TP, None), P(), rows)
    out_specs = (rows, rows, rows, rows, P(TP + SEQ, None))
    return jax.shard_map(
        on_device, mesh=split, in_specs=in_specs, out_specs=out_specs, check_vma=False
    )
```

```python
import functools

import jax
import jax.numpy as jnp
import numpy as np
from jax import lax
from jax.experimental import pallas as pl
from jax.experimental.pallas import tpu as pltpu
from jax.sharding import Mesh
from jax.sharding import PartitionSpec as P

AXES = ("y", "x", "zl", "zh", "c")
SEQ = ("y", "x", "zl")
TP = ("zh", "c")
LEN = 128
MESH = pl.DeviceIdType.MESH
F32 = jnp.float32
BF16 = jnp.bfloat16


def split_hi_lo(mat):
    hi = np.asarray(mat, np.float32).astype(jnp.bfloat16)
    lo = (mat - hi.astype(np.float64)).astype(np.float32).astype(jnp.bfloat16)
    return np.stack([hi, lo])


def dft_tables():
    n = np.arange(LEN)
    ang = 2 * np.pi * np.outer(n, n) / (2 * LEN)
    alt = np.where(n % 2 == 0, 1.0, -1.0)
    fwd = np.concatenate([np.cos(ang), -np.sin(ang)], 0)
    fwd[LEN] = alt
    inv = np.concatenate([np.cos(ang), -np.sin(ang)], 1) / LEN
    inv[:, 0] = 0.5 / LEN
    inv[:, LEN] = alt * (0.5 / LEN)
    return split_hi_lo(fwd), split_hi_lo(inv)


def dot(a, b, dims=((1,), (0,))):
    return lax.dot_general(a, b, (dims, ((), ())), preferred_element_type=F32)


def kernel(
    q_hbm, k_hbm, v_hbm, w_hbm, taps_hbm, seg_ref, cot_hbm, fa_hbm, ia_hbm,
    out_ref, gq_ref, gk_ref, gv_ref, tg_ref,
    q_ref, k_ref, v_ref, w_ref, taps_ref, cot_ref, fa_ref, ia_ref,
    wbuf, prod, prev, tbuf, xbuf, fil, gbuf, ggs, ggr, gfb, gnx, gft,
    tgf, tgs, r1, s2, r2, ss, rs, ls,
):
    y, x, zl, zh, c = (lax.axis_index(a) for a in AXES)
    t = zh * 2 + c
    s = (y * 4 + x) * 4 + zl

    loads = []
    pairs = [(w_hbm, w_ref), (k_hbm, k_ref), (v_hbm, v_ref), (taps_hbm, taps_ref)]
    pairs += [(fa_hbm, fa_ref), (ia_hbm, ia_ref), (q_hbm, q_ref), (cot_hbm, cot_ref)]
    for i, (src, dst) in enumerate(pairs):
        cp = pltpu.make_async_copy(src, dst, ls.at[1 + i])
        cp.start()
        loads.append(cp)

    def shift(v, d):
        return lax.rem(v + (d % 4), 4)

    def zxor(j):
        lo, hi = lax.rem(zl, 2), zl // 2
        lo = 1 - lo if j & 1 else lo
        hi = 1 - hi if j & 2 else hi
        return hi * 2 + lo

    def at_x(d):
        return (y, shift(x, d), zl, zh, c)

    def at_y(d):
        return (shift(y, d), x, zl, zh, c)

    def at_z(j):
        return (y, x, zxor(j), zh, c)

    def at_xz(d, j):
        return (y, shift(x, d), zxor(j), zh, c)

    def at_s(d):
        p = lax.rem(s + (d % 64), 64)
        return (p // 16, lax.rem(p // 4, 4), lax.rem(p, 4), zh, c)

    sibling = (y, x, zl, zh, 1 - c)
    across = (y, x, zl, 1 - zh, c)
    diagonal = (y, x, zl, 1 - zh, 1 - c)

    barrier = pltpu.get_barrier_semaphore()
    partners = [across, diagonal, at_s(1), at_s(63), at_z(3), at_z(2), at_z(1), at_x(2), at_y(2)]
    partners += [at_x(1), at_x(3), at_y(1), at_y(3), sibling]
    partners += [at_xz(d, j) for d in range(1, 4) for j in range(1, 4)]
    for dev in partners:
        pl.semaphore_signal(barrier, inc=1, device_id=dev, device_id_type=MESH)

    keys_of = {}
    sends = []

    def make(key, src, dst, dev):
        i = keys_of.setdefault(key, len(keys_of))
        return pltpu.make_async_remote_copy(
            src_ref=src,
            dst_ref=dst,
            send_sem=ss.at[i],
            recv_sem=rs.at[i],
            device_id=dev,
            device_id_type=MESH,
        )

    def send(key, src, dst, dev):
        cp = make(key, src, dst, dev)
        cp.start()
        sends.append(cp)

    def recv(key, dst, dev):
        make(key, dst, dst, dev).wait_recv()

    for cp in loads[:3]:
        cp.wait()
    own_w = pltpu.make_async_copy(
        w_ref, wbuf.at[pl.ds(pl.multiple_of(s * 64, 64), 64)], ls.at[0]
    )
    own_w.start()
    for i in range(4):
        cols = pl.ds(i * 256, 256)
        prod[:, cols] = (k_ref[:, cols].astype(F32) * v_ref[:, cols].astype(F32)).astype(BF16)

    def chunk(j, a, b, part=None):
        dx, dy = (a, b) if j % 2 == 0 else (b, a)
        off = ((shift(y, dy) * 4 + shift(x, dx)) * 4 + zxor(j)) * 64
        size = 64
        if part is not None:
            off, size = off + 32 * part, 32
        return wbuf.at[pl.ds(pl.multiple_of(off, size), size)]

    def step(j, first, d):
        along_x = (j % 2 == 0) == first
        return at_x(d) if along_x else at_y(d)

    def source(j, a):
        return w_ref if j == 0 and a == 0 else chunk(j, a, 0)

    def second(j, a):
        src = source(j, a)
        send(("u1", j, a), src, chunk(j, a, 0), step(j, False, 1))
        send(("u2", j, a), src, chunk(j, a, 0), step(j, False, -1))

    def s1(j):
        src = source(j, 0)
        send(("t1", j), src, chunk(j, 0, 0), step(j, True, 1))
        send(("t2", j), src, chunk(j, 0, 0), step(j, True, -1))
        second(j, 0)

    def s2_(j):
        recv(("t1", j), chunk(j, -1, 0), step(j, True, 1))
        send(("t3", j), chunk(j, -1, 0, 0), chunk(j, -1, 0, 0), step(j, True, 1))
        recv(("t2", j), chunk(j, 1, 0), step(j, True, -1))
        send(("t4", j), chunk(j, 1, 0, 1), chunk(j, 1, 0, 1), step(j, True, -1))
        second(j, -1)
        second(j, 1)

    def s3_(j):
        recv(("t3", j), chunk(j, 2, 0, 0), step(j, True, 1))
        recv(("t4", j), chunk(j, 2, 0, 1), step(j, True, -1))
        second(j, 2)

    def relay(j, a):
        recv(("u1", j, a), chunk(j, a, -1), step(j, False, 1))
        send(("u3", j, a), chunk(j, a, -1, 0), chunk(j, a, -1, 0), step(j, False, 1))
        recv(("u2", j, a), chunk(j, a, 1), step(j, False, -1))
        send(("u4", j, a), chunk(j, a, 1, 1), chunk(j, a, 1, 1), step(j, False, -1))

    def last(j, a):
        recv(("u3", j, a), chunk(j, a, 2, 0), step(j, False, 1))
        recv(("u4", j, a), chunk(j, a, 2, 1), step(j, False, -1))

    def own_place(j):
        return wbuf.at[pl.ds(pl.multiple_of(((y * 4 + x) * 4 + zxor(j)) * 64, 64), 64)]

    def half_of(p):
        return zl // 2 if p == 0 else 1 - zl // 2

    def gg_copy(p, dy):
        yy, h = shift(y, dy), half_of(p)
        delta = lax.rem(yy + 4 - t, 4)
        i = gg_base + p * 4 + delta
        return delta, pltpu.make_async_remote_copy(
            src_ref=ggs.at[yy, h],
            dst_ref=ggr.at[delta, h],
            send_sem=ss.at[i],
            recv_sem=rs.at[i],
            device_id=(y, x, zl, yy // 2, lax.rem(yy, 2)),
            device_id_type=MESH,
        )

    def batch(p, dy):
        yy, h = shift(y, dy), half_of(p)

        def one(i, carry):
            rows = pl.ds(pl.multiple_of(yy * 1024 + i * 256 + h * 128, 128), 128)
            part = dot(cot_ref[...], wbuf[rows, :], ((1,), (1,)))
            ggs[yy, h, i] = part.astype(BF16)
            return carry

        lax.fori_loop(0, 4, one, 0, unroll=True)
        delta, cp = gg_copy(p, dy)

        @pl.when(delta != 0)
        def _():
            cp.start()

    gg_base = 160
    halo_base = 168

    row = lax.broadcasted_iota(jnp.int32, (2 * LEN, 128), 0)
    sign = (1 - 2 * lax.rem(row, 2)).astype(F32)
    inner = lax.broadcasted_iota(jnp.int32, (LEN, 128), 0) != 0

    def dft(val):
        return dot(fa_ref[0], val) + dot(fa_ref[1], val)

    def idft(val):
        hi = val.astype(BF16)
        lo = (val - hi.astype(F32)).astype(BF16)
        return dot(ia_ref[0], hi) + dot(ia_ref[0], lo) + dot(ia_ref[1], hi)

    def cmul(a, b, conj):
        ar, ai, br, bi = a[:LEN], a[LEN:], b[:LEN], b[LEN:]
        ii = ai * bi
        if conj:
            re = ar * br + jnp.where(inner, ii, 0.0)
            im = jnp.where(inner, ai * br - ar * bi, ii)
        else:
            re = ar * br - jnp.where(inner, ii, 0.0)
            im = jnp.where(inner, ai * br + ar * bi, ii)
        return jnp.concatenate([re, im], 0)

    def strips(fn):
        def one(e, carry):
            fn(e, pl.ds(pl.multiple_of(e * 128, 128), 128))
            return carry

        lax.fori_loop(0, 8, one, 0, unroll=True)

    here = seg_ref[s]
    back = seg_ref[jnp.maximum(s - 1, 0)]
    ahead = seg_ref[jnp.minimum(s + 1, 63)]
    linked = jnp.where(jnp.logical_and(s > 0, here == back), 1.0, 0.0).astype(F32)
    linked_next = jnp.where(jnp.logical_and(s < 63, here == ahead), 1.0, 0.0).astype(F32)

    def rows_of(place, size):
        return pl.ds(pl.multiple_of(place * size, size), size)

    def half_copy(base, h, src, dst, dev):
        return pltpu.make_async_remote_copy(
            src_ref=src,
            dst_ref=dst,
            send_sem=ss.at[base + h],
            recv_sem=rs.at[base + h],
            device_id=dev,
            device_id_type=MESH,
        )

    def half_tail(p):
        h = half_of(p)
        for delta in range(1, 4):
            i = gg_base + p * 4 + delta
            pltpu.make_async_remote_copy(
                src_ref=ggr.at[delta, h],
                dst_ref=ggr.at[delta, h],
                send_sem=ss.at[i],
                recv_sem=rs.at[i],
                device_id=sibling,
                device_id_type=MESH,
            ).wait_recv()

        def cols_of(i):
            return pl.ds(pl.multiple_of(i * 256 + h * 128, 128), 128)

        def gradients(i, carry):
            cols = cols_of(i)
            total = ggs[t, h, i].astype(F32)
            for delta in range(1, 4):
                total = total + ggr[delta, h, i].astype(F32)
            gg = total.astype(BF16).astype(F32)
            gfb[h, i] = (gg * q_ref[:, cols].astype(F32)).astype(BF16)
            gq_ref[:, cols] = (gg * fil[:, cols].astype(F32)).astype(BF16)
            return carry

        lax.fori_loop(0, 4, gradients, 0, unroll=True)
        half_copy(halo_base, h, gfb.at[h], gnx.at[h], at_s(-1)).start()

        def taps_part(i, carry):
            cols = cols_of(i)
            spec = dft(gfb[h, i])
            e = i * 2 + h
            gft[e] = spec
            part = idft(cmul(spec, xbuf[e], True)).T
            tgf[cols, :] = part
            tgs[cols, :] = part.astype(BF16)
            return carry

        lax.fori_loop(0, 4, taps_part, 0, unroll=True)
        for d in (2, 1, 3):
            rows = pl.ds(pl.multiple_of(shift(y, d) * 256 + h * 128, 128), 128)
            here = pl.ds(pl.multiple_of(h * 128, 128), 128)
            send(("r1", p, d), tgs.at[rows], r1.at[d - 1, here], at_y(d))

    def r1_rows(p):
        return pl.ds(pl.multiple_of(half_of(p) * 128, 128), 128)

    def backward(h):
        half_copy(halo_base, h, gfb.at[h], gnx.at[h], at_s(-1)).wait_recv()

        def one(i, carry):
            e = i * 2 + h
            cols = pl.ds(pl.multiple_of(e * 128, 128), 128)
            spec = gft[e] + linked_next * (sign * dft(gnx[h, i]))
            gp = idft(cmul(spec, tbuf[e], True)).astype(BF16).astype(F32)
            gk_ref[:, cols] = (gp * v_ref[:, cols].astype(F32)).astype(BF16)
            gv_ref[:, cols] = (gp * k_ref[:, cols].astype(F32)).astype(BF16)
            return carry

        lax.fori_loop(0, 4, one, 0, unroll=True)

    for cp in loads[3:]:
        cp.wait()
    pl.semaphore_wait(barrier, len(partners))

    s1(0)
    send("z1", w_ref, own_place(0), at_z(1))
    send("z2", w_ref, own_place(0), at_z(2))
    send("halo", prod, prev, at_s(1))

    def spectra(e, cols):
        tap = taps_ref[cols, :]
        tbuf[e] = dot(fa_ref[0], tap, ((1,), (1,))) + dot(fa_ref[1], tap, ((1,), (1,)))
        xbuf[e] = dft(prod[:, cols])

    strips(spectra)
    own_w.wait()

    recv("z1", own_place(1), at_z(1))
    send("z3", own_place(1), own_place(1), at_z(2))
    s1(1)
    s2_(0)
    s2_(1)
    s3_(0)
    s3_(1)
    relay(0, 0)
    relay(1, 0)
    recv("z2", own_place(2), at_z(2))
    s1(2)
    recv("halo", prev, at_s(1))

    def forward(e, cols):
        spec = xbuf[e] + linked * (sign * dft(prev[:, cols]))
        xbuf[e] = spec
        filt = idft(cmul(spec, tbuf[e], False)).astype(BF16)
        fil[:, cols] = filt
        gbuf[t, :, cols] = (q_ref[:, cols].astype(F32) * filt.astype(F32)).astype(BF16)

    strips(forward)
    t_sib, t_acr, t_dia = zh * 2 + 1 - c, (1 - zh) * 2 + c, (1 - zh) * 2 + 1 - c
    send("g2", gbuf.at[t], gbuf.at[t], across)
    send("g1", gbuf.at[t], gbuf.at[t], sibling)

    relay(0, -1)
    relay(1, -1)
    relay(0, 1)
    relay(1, 1)
    recv("z3", own_place(3), at_z(2))
    s1(3)
    s2_(2)
    relay(0, 2)
    relay(1, 2)
    s2_(3)
    last(0, 0)
    last(1, 0)
    batch(0, 0)
    s3_(2)
    s3_(3)
    relay(2, 0)
    relay(3, 0)
    for a in (-1, 1):
        last(0, a)
        last(1, a)
    last(0, 2)
    batch(0, -1)
    relay(2, -1)
    relay(3, -1)
    batch(0, 1)
    relay(2, 1)
    relay(3, 1)
    last(1, 2)
    batch(0, 2)
    relay(2, 2)
    relay(3, 2)
    recv("g2", gbuf.at[t_acr], across)
    send("g3", gbuf.at[t_acr], gbuf.at[t_acr], sibling)
    last(2, 0)
    last(3, 0)
    batch(1, 0)
    half_tail(0)
    for a in (-1, 1):
        last(2, a)
        last(3, a)
    last(2, 2)
    batch(1, -1)
    batch(1, 1)
    last(3, 2)
    batch(1, 2)

    recv("g1", gbuf.at[t_sib], sibling)
    recv("g3", gbuf.at[t_dia], sibling)

    def outputs(n):
        cols = pl.ds(n * 256, 256)
        total = dot(gbuf[0], wbuf[0:1024, cols])
        for i in range(1, 4):
            total = total + dot(gbuf[i], wbuf[i * 1024 : (i + 1) * 1024, cols])
        out_ref[:, cols] = total.astype(BF16)

    for n in range(4):
        outputs(n)

    @pl.when(lax.rem(zl, 2) == 0)
    def _():
        backward(half_of(0))

    half_tail(1)
    for p in range(2):
        for d in range(1, 4):
            recv(("r1", p, d), r1.at[d - 1, r1_rows(p)], at_y(d))
    total = tgf[rows_of(y, 256), :]
    for d in range(3):
        total = total + r1[d].astype(F32)
    s2[...] = total
    for d in (2, 1, 3, 0):
        for j in (3, 2, 1, 0):
            if d or j:
                rows = rows_of(shift(x, d) * 4 + zxor(j), 16)
                send(("r2", d, j), s2.at[rows], r2.at[d * 4 + j], at_xz(d, j))

    backward(half_of(1))

    @pl.when(lax.rem(zl, 2) == 1)
    def _():
        backward(half_of(0))

    total = s2[rows_of(x * 4 + zl, 16), :]
    for d in range(4):
        for j in range(4):
            if d or j:
                recv(("r2", d, j), r2.at[d * 4 + j], at_xz(d, j))
                total = total + r2[d * 4 + j]
    tg_ref[...] = total

    for h in range(2):
        half_copy(halo_base, h, gfb.at[h], gnx.at[h], at_s(-1)).wait_send()
    for cp in sends:
        cp.wait_send()
    for p in range(2):
        for dy in (0, -1, 1, 2):
            delta, cp = gg_copy(p, dy)

            @pl.when(delta != 0)
            def _(cp=cp):
                cp.wait_send()

    assert len(keys_of) <= gg_base


def write_out(*refs):
    ins, outs, bufs, sem = refs[:5], refs[5:10], refs[10:15], refs[15]
    reads = [pltpu.make_async_copy(ins[i], bufs[i], sem.at[i]) for i in range(5)]
    writes = [pltpu.make_async_copy(bufs[i], outs[i], sem.at[5 + i]) for i in range(5)]
    for cp in reads:
        cp.start()
    for read, write in zip(reads, writes):
        read.wait()
        write.start()
    for cp in writes:
        cp.wait()


def on_device(queries, keys, values, w_out, taps, seg_ids, cotangent):
    fwd, inv = dft_tables()
    block = queries.shape
    vmem = pl.BlockSpec(memory_space=pltpu.VMEM)
    hbm = pl.BlockSpec(memory_space=pl.ANY)
    smem = pl.BlockSpec(memory_space=pltpu.SMEM)
    outs = [jax.ShapeDtypeStruct(block, BF16)] * 4 + [jax.ShapeDtypeStruct((16, LEN), F32)]
    scratch = [
        pltpu.VMEM(block, BF16),
        pltpu.VMEM(block, BF16),
        pltpu.VMEM(block, BF16),
        pltpu.VMEM((64, 1024), BF16),
        pltpu.VMEM((1024, LEN), BF16),
        pltpu.VMEM(block, BF16),
        pltpu.VMEM((2, 256, 128), BF16),
        pltpu.VMEM((2, 128, 256), BF16),
        pltpu.VMEM((4096, 1024), BF16),
        pltpu.VMEM(block, BF16),
        pltpu.VMEM(block, BF16),
        pltpu.VMEM((8, 256, 128), F32),
        pltpu.VMEM((8, 256, 128), F32),
        pltpu.VMEM(block, BF16),
        pltpu.VMEM((4, *block), BF16),
        pltpu.VMEM((4, 2, 4, 128, 128), BF16),
        pltpu.VMEM((4, 2, 4, 128, 128), BF16),
        pltpu.VMEM((2, 4, 128, 128), BF16),
        pltpu.VMEM((2, 4, 128, 128), BF16),
        pltpu.VMEM((8, 256, 128), F32),
        pltpu.VMEM((1024, LEN), F32),
        pltpu.VMEM((1024, LEN), BF16),
        pltpu.VMEM((3, 256, LEN), BF16),
        pltpu.VMEM((256, LEN), F32),
        pltpu.VMEM((16, 16, LEN), F32),
        pltpu.SemaphoreType.DMA((170,)),
        pltpu.SemaphoreType.DMA((170,)),
        pltpu.SemaphoreType.DMA((9,)),
    ]
    results = pl.pallas_call(
        kernel,
        out_shape=outs,
        in_specs=[hbm] * 5 + [smem] + [hbm] * 3,
        out_specs=[vmem] * 5,
        scratch_shapes=scratch,
        compiler_params=pltpu.CompilerParams(
            collective_id=0, has_side_effects=True, vmem_limit_bytes=67043328
        ),
        name="hyena",
    )(queries, keys, values, w_out, taps, seg_ids, cotangent, jnp.asarray(fwd), jnp.asarray(inv))
    return pl.pallas_call(
        write_out,
        out_shape=outs,
        in_specs=[hbm] * 5,
        out_specs=[hbm] * 5,
        scratch_shapes=[pltpu.VMEM(o.shape, o.dtype) for o in outs]
        + [pltpu.SemaphoreType.DMA((10,))],
        compiler_params=pltpu.CompilerParams(vmem_limit_bytes=67043328),
        name="write_out",
    )(*results)


def solution(mesh):
    split = Mesh(mesh.devices.reshape(4, 4, 4, 2, 2), AXES)
    rows = P(SEQ, TP)
    in_specs = (rows, rows, rows, rows, P(TP, None), P(), rows)
    out_specs = (rows, rows, rows, rows, P(TP + SEQ, None))
    return jax.shard_map(
        on_device, mesh=split, in_specs=in_specs, out_specs=out_specs, check_vma=False
    )
```

```python
import functools

import jax
import jax.numpy as jnp
import numpy as np
from jax import lax
from jax.experimental import pallas as pl
from jax.experimental.pallas import tpu as pltpu
from jax.sharding import Mesh
from jax.sharding import PartitionSpec as P

AXES = ("y", "x", "zl", "zh", "c")
SEQ = ("y", "x", "zl")
TP = ("zh", "c")
LEN = 128
MESH = pl.DeviceIdType.MESH
F32 = jnp.float32
BF16 = jnp.bfloat16


def split_hi_lo(mat):
    hi = np.asarray(mat, np.float32).astype(jnp.bfloat16)
    lo = (mat - hi.astype(np.float64)).astype(np.float32).astype(jnp.bfloat16)
    return np.stack([hi, lo])


def dft_tables():
    n = np.arange(LEN)
    ang = 2 * np.pi * np.outer(n, n) / (2 * LEN)
    alt = np.where(n % 2 == 0, 1.0, -1.0)
    fwd = np.concatenate([np.cos(ang), -np.sin(ang)], 0)
    fwd[LEN] = alt
    inv = np.concatenate([np.cos(ang), -np.sin(ang)], 1) / LEN
    inv[:, 0] = 0.5 / LEN
    inv[:, LEN] = alt * (0.5 / LEN)
    return split_hi_lo(fwd), split_hi_lo(inv)


def dot(a, b, dims=((1,), (0,))):
    return lax.dot_general(a, b, (dims, ((), ())), preferred_element_type=F32)


def kernel(
    q_hbm, k_hbm, v_hbm, w_hbm, taps_hbm, seg_ref, cot_hbm, fa_hbm, ia_hbm,
    out_ref, gq_ref, gk_ref, gv_ref, tg_ref,
    q_ref, k_ref, v_ref, w_ref, taps_ref, cot_ref, fa_ref, ia_ref,
    wbuf, prod, prev, tbuf, xbuf, fil, gbuf, ggs, ggr, gfb, gnx, gft,
    tgf, tgs, r1, s2, r2, ss, rs, ls,
):
    y, x, zl, zh, c = (lax.axis_index(a) for a in AXES)
    t = zh * 2 + c
    s = (y * 4 + x) * 4 + zl

    loads = []
    pairs = [(w_hbm, w_ref), (k_hbm, k_ref), (v_hbm, v_ref), (taps_hbm, taps_ref)]
    pairs += [(fa_hbm, fa_ref), (ia_hbm, ia_ref), (q_hbm, q_ref), (cot_hbm, cot_ref)]
    for i, (src, dst) in enumerate(pairs):
        cp = pltpu.make_async_copy(src, dst, ls.at[1 + i])
        cp.start()
        loads.append(cp)

    def shift(v, d):
        return lax.rem(v + (d % 4), 4)

    def zxor(j):
        lo, hi = lax.rem(zl, 2), zl // 2
        lo = 1 - lo if j & 1 else lo
        hi = 1 - hi if j & 2 else hi
        return hi * 2 + lo

    def at_x(d):
        return (y, shift(x, d), zl, zh, c)

    def at_y(d):
        return (shift(y, d), x, zl, zh, c)

    def at_z(j):
        return (y, x, zxor(j), zh, c)

    def at_xz(d, j):
        return (y, shift(x, d), zxor(j), zh, c)

    def at_s(d):
        p = lax.rem(s + (d % 64), 64)
        return (p // 16, lax.rem(p // 4, 4), lax.rem(p, 4), zh, c)

    sibling = (y, x, zl, zh, 1 - c)
    across = (y, x, zl, 1 - zh, c)
    diagonal = (y, x, zl, 1 - zh, 1 - c)

    barrier = pltpu.get_barrier_semaphore()
    partners = [across, diagonal, at_s(1), at_s(63), at_z(3), at_z(2), at_z(1), at_x(2), at_y(2)]
    partners += [at_x(1), at_x(3), at_y(1), at_y(3), sibling]
    partners += [at_xz(d, j) for d in range(1, 4) for j in range(1, 4)]
    for dev in partners:
        pl.semaphore_signal(barrier, inc=1, device_id=dev, device_id_type=MESH)

    keys_of = {}
    sends = []

    def make(key, src, dst, dev):
        i = keys_of.setdefault(key, len(keys_of))
        return pltpu.make_async_remote_copy(
            src_ref=src,
            dst_ref=dst,
            send_sem=ss.at[i],
            recv_sem=rs.at[i],
            device_id=dev,
            device_id_type=MESH,
        )

    def send(key, src, dst, dev):
        cp = make(key, src, dst, dev)
        cp.start()
        sends.append(cp)

    def recv(key, dst, dev):
        make(key, dst, dst, dev).wait_recv()

    for cp in loads[:3]:
        cp.wait()
    own_w = pltpu.make_async_copy(
        w_ref, wbuf.at[pl.ds(pl.multiple_of(s * 64, 64), 64)], ls.at[0]
    )
    own_w.start()
    for i in range(4):
        cols = pl.ds(i * 256, 256)
        prod[:, cols] = (k_ref[:, cols].astype(F32) * v_ref[:, cols].astype(F32)).astype(BF16)

    def chunk(j, a, b, part=None):
        dx, dy = (a, b) if j % 2 == 0 else (b, a)
        off = ((shift(y, dy) * 4 + shift(x, dx)) * 4 + zxor(j)) * 64
        size = 64
        if part is not None:
            off, size = off + 32 * part, 32
        return wbuf.at[pl.ds(pl.multiple_of(off, size), size)]

    def step(j, first, d):
        along_x = (j % 2 == 0) == first
        return at_x(d) if along_x else at_y(d)

    def source(j, a):
        return w_ref if j == 0 and a == 0 else chunk(j, a, 0)

    def second(j, a):
        src = source(j, a)
        send(("u1", j, a), src, chunk(j, a, 0), step(j, False, 1))
        send(("u2", j, a), src, chunk(j, a, 0), step(j, False, -1))

    def s1(j):
        src = source(j, 0)
        send(("t1", j), src, chunk(j, 0, 0), step(j, True, 1))
        send(("t2", j), src, chunk(j, 0, 0), step(j, True, -1))
        second(j, 0)

    def s2_(j):
        recv(("t1", j), chunk(j, -1, 0), step(j, True, 1))
        send(("t3", j), chunk(j, -1, 0, 0), chunk(j, -1, 0, 0), step(j, True, 1))
        recv(("t2", j), chunk(j, 1, 0), step(j, True, -1))
        send(("t4", j), chunk(j, 1, 0, 1), chunk(j, 1, 0, 1), step(j, True, -1))
        second(j, -1)
        second(j, 1)

    def s3_(j):
        recv(("t3", j), chunk(j, 2, 0, 0), step(j, True, 1))
        recv(("t4", j), chunk(j, 2, 0, 1), step(j, True, -1))
        second(j, 2)

    def relay(j, a):
        recv(("u1", j, a), chunk(j, a, -1), step(j, False, 1))
        send(("u3", j, a), chunk(j, a, -1, 0), chunk(j, a, -1, 0), step(j, False, 1))
        recv(("u2", j, a), chunk(j, a, 1), step(j, False, -1))
        send(("u4", j, a), chunk(j, a, 1, 1), chunk(j, a, 1, 1), step(j, False, -1))

    def last(j, a):
        recv(("u3", j, a), chunk(j, a, 2, 0), step(j, False, 1))
        recv(("u4", j, a), chunk(j, a, 2, 1), step(j, False, -1))

    def own_place(j):
        return wbuf.at[pl.ds(pl.multiple_of(((y * 4 + x) * 4 + zxor(j)) * 64, 64), 64)]

    def half_of(p):
        return zl // 2 if p == 0 else 1 - zl // 2

    def gg_copy(p, dy):
        yy, h = shift(y, dy), half_of(p)
        delta = lax.rem(yy + 4 - t, 4)
        i = gg_base + p * 4 + delta
        return delta, pltpu.make_async_remote_copy(
            src_ref=ggs.at[yy, h],
            dst_ref=ggr.at[delta, h],
            send_sem=ss.at[i],
            recv_sem=rs.at[i],
            device_id=(y, x, zl, yy // 2, lax.rem(yy, 2)),
            device_id_type=MESH,
        )

    def batch(p, dy):
        yy, h = shift(y, dy), half_of(p)

        def one(i, carry):
            rows = pl.ds(pl.multiple_of(yy * 1024 + i * 256 + h * 128, 128), 128)
            part = dot(cot_ref[...], wbuf[rows, :], ((1,), (1,)))
            ggs[yy, h, i] = part.astype(BF16)
            return carry

        lax.fori_loop(0, 4, one, 0, unroll=True)
        delta, cp = gg_copy(p, dy)

        @pl.when(delta != 0)
        def _():
            cp.start()

    gg_base = 160
    halo_base = 168

    row = lax.broadcasted_iota(jnp.int32, (2 * LEN, 128), 0)
    sign = (1 - 2 * lax.rem(row, 2)).astype(F32)
    inner = lax.broadcasted_iota(jnp.int32, (LEN, 128), 0) != 0

    def dft(val):
        return dot(fa_ref[0], val) + dot(fa_ref[1], val)

    def idft(val):
        hi = val.astype(BF16)
        lo = (val - hi.astype(F32)).astype(BF16)
        return dot(ia_ref[0], hi) + dot(ia_ref[0], lo) + dot(ia_ref[1], hi)

    def cmul(a, b, conj):
        ar, ai, br, bi = a[:LEN], a[LEN:], b[:LEN], b[LEN:]
        ii = ai * bi
        if conj:
            re = ar * br + jnp.where(inner, ii, 0.0)
            im = jnp.where(inner, ai * br - ar * bi, ii)
        else:
            re = ar * br - jnp.where(inner, ii, 0.0)
            im = jnp.where(inner, ai * br + ar * bi, ii)
        return jnp.concatenate([re, im], 0)

    def strips(fn):
        def one(e, carry):
            fn(e, pl.ds(pl.multiple_of(e * 128, 128), 128))
            return carry

        lax.fori_loop(0, 8, one, 0, unroll=True)

    here = seg_ref[s]
    back = seg_ref[jnp.maximum(s - 1, 0)]
    ahead = seg_ref[jnp.minimum(s + 1, 63)]
    linked = jnp.where(jnp.logical_and(s > 0, here == back), 1.0, 0.0).astype(F32)
    linked_next = jnp.where(jnp.logical_and(s < 63, here == ahead), 1.0, 0.0).astype(F32)

    def rows_of(place, size):
        return pl.ds(pl.multiple_of(place * size, size), size)

    def half_copy(base, h, src, dst, dev):
        return pltpu.make_async_remote_copy(
            src_ref=src,
            dst_ref=dst,
            send_sem=ss.at[base + h],
            recv_sem=rs.at[base + h],
            device_id=dev,
            device_id_type=MESH,
        )

    def half_tail(p):
        h = half_of(p)
        for delta in range(1, 4):
            i = gg_base + p * 4 + delta
            pltpu.make_async_remote_copy(
                src_ref=ggr.at[delta, h],
                dst_ref=ggr.at[delta, h],
                send_sem=ss.at[i],
                recv_sem=rs.at[i],
                device_id=sibling,
                device_id_type=MESH,
            ).wait_recv()

        def cols_of(i):
            return pl.ds(pl.multiple_of(i * 256 + h * 128, 128), 128)

        def gradients(i, carry):
            cols = cols_of(i)
            total = ggs[t, h, i].astype(F32)
            for delta in range(1, 4):
                total = total + ggr[delta, h, i].astype(F32)
            gg = total.astype(BF16).astype(F32)
            gfb[h, i] = (gg * q_ref[:, cols].astype(F32)).astype(BF16)
            gq_ref[:, cols] = (gg * fil[:, cols].astype(F32)).astype(BF16)
            return carry

        lax.fori_loop(0, 4, gradients, 0, unroll=True)
        half_copy(halo_base, h, gfb.at[h], gnx.at[h], at_s(-1)).start()

        def taps_part(i, carry):
            cols = cols_of(i)
            spec = dft(gfb[h, i])
            e = i * 2 + h
            gft[e] = spec
            part = idft(cmul(spec, xbuf[e], True)).T
            tgf[cols, :] = part
            tgs[cols, :] = part.astype(BF16)
            return carry

        lax.fori_loop(0, 4, taps_part, 0, unroll=True)
        for d in (2, 1, 3):
            rows = pl.ds(pl.multiple_of(shift(y, d) * 256 + h * 128, 128), 128)
            here = pl.ds(pl.multiple_of(h * 128, 128), 128)
            send(("r1", p, d), tgs.at[rows], r1.at[d - 1, here], at_y(d))

    def r1_rows(p):
        return pl.ds(pl.multiple_of(half_of(p) * 128, 128), 128)

    def backward(h):
        half_copy(halo_base, h, gfb.at[h], gnx.at[h], at_s(-1)).wait_recv()

        def one(i, carry):
            e = i * 2 + h
            cols = pl.ds(pl.multiple_of(e * 128, 128), 128)
            spec = gft[e] + linked_next * (sign * dft(gnx[h, i]))
            gp = idft(cmul(spec, tbuf[e], True)).astype(BF16).astype(F32)
            gk_ref[:, cols] = (gp * v_ref[:, cols].astype(F32)).astype(BF16)
            gv_ref[:, cols] = (gp * k_ref[:, cols].astype(F32)).astype(BF16)
            return carry

        lax.fori_loop(0, 4, one, 0, unroll=True)

    for cp in loads[3:]:
        cp.wait()
    pl.semaphore_wait(barrier, len(partners))

    s1(0)
    send("z1", w_ref, own_place(0), at_z(1))
    send("z2", w_ref, own_place(0), at_z(2))
    send("halo", prod, prev, at_s(1))

    def spectra(e, cols):
        tap = taps_ref[cols, :]
        tbuf[e] = dot(fa_ref[0], tap, ((1,), (1,))) + dot(fa_ref[1], tap, ((1,), (1,)))
        xbuf[e] = dft(prod[:, cols])

    strips(spectra)
    own_w.wait()

    recv("z1", own_place(1), at_z(1))
    send("z3", own_place(1), own_place(1), at_z(2))
    s1(1)
    s2_(0)
    s2_(1)
    s3_(0)
    s3_(1)
    relay(0, 0)
    relay(1, 0)
    recv("z2", own_place(2), at_z(2))
    s1(2)
    recv("halo", prev, at_s(1))

    def forward(e, cols):
        spec = xbuf[e] + linked * (sign * dft(prev[:, cols]))
        xbuf[e] = spec
        filt = idft(cmul(spec, tbuf[e], False)).astype(BF16)
        fil[:, cols] = filt
        gbuf[t, :, cols] = (q_ref[:, cols].astype(F32) * filt.astype(F32)).astype(BF16)

    strips(forward)
    t_sib, t_acr, t_dia = zh * 2 + 1 - c, (1 - zh) * 2 + c, (1 - zh) * 2 + 1 - c
    send("g2", gbuf.at[t], gbuf.at[t], across)
    send("g1", gbuf.at[t], gbuf.at[t], sibling)

    relay(0, -1)
    relay(1, -1)
    relay(0, 1)
    relay(1, 1)
    recv("z3", own_place(3), at_z(2))
    s1(3)
    s2_(2)
    relay(0, 2)
    relay(1, 2)
    s2_(3)
    last(0, 0)
    last(1, 0)
    batch(0, 0)
    s3_(2)
    s3_(3)
    relay(2, 0)
    relay(3, 0)
    for a in (-1, 1):
        last(0, a)
        last(1, a)
    last(0, 2)
    batch(0, -1)
    relay(2, -1)
    relay(3, -1)
    batch(0, 1)
    relay(2, 1)
    relay(3, 1)
    last(1, 2)
    batch(0, 2)
    relay(2, 2)
    relay(3, 2)
    last(2, 0)
    last(3, 0)
    batch(1, 0)
    for a in (-1, 1):
        last(2, a)
        last(3, a)
    last(2, 2)
    batch(1, -1)
    batch(1, 1)
    last(3, 2)
    batch(1, 2)

    half_tail(0)
    recv("g2", gbuf.at[t_acr], across)
    send("g3", gbuf.at[t_acr], gbuf.at[t_acr], sibling)
    half_tail(1)

    @pl.when(lax.rem(zl, 2) == 0)
    def _():
        backward(half_of(0))

    def outputs(n):
        cols = pl.ds(n * 256, 256)
        total = dot(gbuf[0], wbuf[0:1024, cols])
        for i in range(1, 4):
            total = total + dot(gbuf[i], wbuf[i * 1024 : (i + 1) * 1024, cols])
        out_ref[:, cols] = total.astype(BF16)

    for p in range(2):
        for d in range(1, 4):
            recv(("r1", p, d), r1.at[d - 1, r1_rows(p)], at_y(d))
    total = tgf[rows_of(y, 256), :]
    for d in range(3):
        total = total + r1[d].astype(F32)
    s2[...] = total
    for d in (2, 1, 3, 0):
        for j in (3, 2, 1, 0):
            if d or j:
                rows = rows_of(shift(x, d) * 4 + zxor(j), 16)
                send(("r2", d, j), s2.at[rows], r2.at[d * 4 + j], at_xz(d, j))

    recv("g1", gbuf.at[t_sib], sibling)
    recv("g3", gbuf.at[t_dia], sibling)
    for n in range(4):
        outputs(n)
    backward(half_of(1))

    @pl.when(lax.rem(zl, 2) == 1)
    def _():
        backward(half_of(0))

    total = s2[rows_of(x * 4 + zl, 16), :]
    for d in range(4):
        for j in range(4):
            if d or j:
                recv(("r2", d, j), r2.at[d * 4 + j], at_xz(d, j))
                total = total + r2[d * 4 + j]
    tg_ref[...] = total

    for h in range(2):
        half_copy(halo_base, h, gfb.at[h], gnx.at[h], at_s(-1)).wait_send()
    for cp in sends:
        cp.wait_send()
    for p in range(2):
        for dy in (0, -1, 1, 2):
            delta, cp = gg_copy(p, dy)

            @pl.when(delta != 0)
            def _(cp=cp):
                cp.wait_send()

    assert len(keys_of) <= gg_base


def write_out(*refs):
    ins, outs, bufs, sem = refs[:5], refs[5:10], refs[10:15], refs[15]
    reads = [pltpu.make_async_copy(ins[i], bufs[i], sem.at[i]) for i in range(5)]
    writes = [pltpu.make_async_copy(bufs[i], outs[i], sem.at[5 + i]) for i in range(5)]
    for cp in reads:
        cp.start()
    for read, write in zip(reads, writes):
        read.wait()
        write.start()
    for cp in writes:
        cp.wait()


def on_device(queries, keys, values, w_out, taps, seg_ids, cotangent):
    fwd, inv = dft_tables()
    block = queries.shape
    vmem = pl.BlockSpec(memory_space=pltpu.VMEM)
    hbm = pl.BlockSpec(memory_space=pl.ANY)
    smem = pl.BlockSpec(memory_space=pltpu.SMEM)
    outs = [jax.ShapeDtypeStruct(block, BF16)] * 4 + [jax.ShapeDtypeStruct((16, LEN), F32)]
    scratch = [
        pltpu.VMEM(block, BF16),
        pltpu.VMEM(block, BF16),
        pltpu.VMEM(block, BF16),
        pltpu.VMEM((64, 1024), BF16),
        pltpu.VMEM((1024, LEN), BF16),
        pltpu.VMEM(block, BF16),
        pltpu.VMEM((2, 256, 128), BF16),
        pltpu.VMEM((2, 128, 256), BF16),
        pltpu.VMEM((4096, 1024), BF16),
        pltpu.VMEM(block, BF16),
        pltpu.VMEM(block, BF16),
        pltpu.VMEM((8, 256, 128), F32),
        pltpu.VMEM((8, 256, 128), F32),
        pltpu.VMEM(block, BF16),
        pltpu.VMEM((4, *block), BF16),
        pltpu.VMEM((4, 2, 4, 128, 128), BF16),
        pltpu.VMEM((4, 2, 4, 128, 128), BF16),
        pltpu.VMEM((2, 4, 128, 128), BF16),
        pltpu.VMEM((2, 4, 128, 128), BF16),
        pltpu.VMEM((8, 256, 128), F32),
        pltpu.VMEM((1024, LEN), F32),
        pltpu.VMEM((1024, LEN), BF16),
        pltpu.VMEM((3, 256, LEN), BF16),
        pltpu.VMEM((256, LEN), F32),
        pltpu.VMEM((16, 16, LEN), F32),
        pltpu.SemaphoreType.DMA((170,)),
        pltpu.SemaphoreType.DMA((170,)),
        pltpu.SemaphoreType.DMA((9,)),
    ]
    results = pl.pallas_call(
        kernel,
        out_shape=outs,
        in_specs=[hbm] * 5 + [smem] + [hbm] * 3,
        out_specs=[vmem] * 5,
        scratch_shapes=scratch,
        compiler_params=pltpu.CompilerParams(
            collective_id=0, has_side_effects=True, vmem_limit_bytes=67043328
        ),
        name="hyena",
    )(queries, keys, values, w_out, taps, seg_ids, cotangent, jnp.asarray(fwd), jnp.asarray(inv))
    return pl.pallas_call(
        write_out,
        out_shape=outs,
        in_specs=[hbm] * 5,
        out_specs=[hbm] * 5,
        scratch_shapes=[pltpu.VMEM(o.shape, o.dtype) for o in outs]
        + [pltpu.SemaphoreType.DMA((10,))],
        compiler_params=pltpu.CompilerParams(vmem_limit_bytes=67043328),
        name="write_out",
    )(*results)


def solution(mesh):
    split = Mesh(mesh.devices.reshape(4, 4, 4, 2, 2), AXES)
    rows = P(SEQ, TP)
    in_specs = (rows, rows, rows, rows, P(TP, None), P(), rows)
    out_specs = (rows, rows, rows, rows, P(TP + SEQ, None))
    return jax.shard_map(
        on_device, mesh=split, in_specs=in_specs, out_specs=out_specs, check_vma=False
    )
```

```python
import functools

import jax
import jax.numpy as jnp
import numpy as np
from jax import lax
from jax.experimental import pallas as pl
from jax.experimental.pallas import tpu as pltpu
from jax.sharding import Mesh
from jax.sharding import PartitionSpec as P

AXES = ("y", "x", "zl", "zh", "c")
SEQ = ("y", "x", "zl")
TP = ("zh", "c")
LEN = 128
MESH = pl.DeviceIdType.MESH
F32 = jnp.float32
BF16 = jnp.bfloat16


def split_hi_lo(mat):
    hi = np.asarray(mat, np.float32).astype(jnp.bfloat16)
    lo = (mat - hi.astype(np.float64)).astype(np.float32).astype(jnp.bfloat16)
    return np.stack([hi, lo])


def dft_tables():
    n = np.arange(LEN)
    ang = 2 * np.pi * np.outer(n, n) / (2 * LEN)
    alt = np.where(n % 2 == 0, 1.0, -1.0)
    fwd = np.concatenate([np.cos(ang), -np.sin(ang)], 0)
    fwd[LEN] = alt
    inv = np.concatenate([np.cos(ang), -np.sin(ang)], 1) / LEN
    inv[:, 0] = 0.5 / LEN
    inv[:, LEN] = alt * (0.5 / LEN)
    return split_hi_lo(fwd), split_hi_lo(inv)


def dot(a, b, dims=((1,), (0,))):
    return lax.dot_general(a, b, (dims, ((), ())), preferred_element_type=F32)


def kernel(
    q_hbm, k_hbm, v_hbm, w_hbm, taps_hbm, seg_ref, cot_hbm, fa_hbm, ia_hbm,
    out_ref, gq_ref, gk_ref, gv_ref, tg_ref,
    q_ref, k_ref, v_ref, w_ref, taps_ref, cot_ref, fa_ref, ia_ref,
    wbuf, prod, prev, tbuf, xbuf, fil, gbuf, ggs, ggr, gs0, ga0, x0, xs, gfb, gnx, gft,
    tgf, tgs, r1, s2, r2, ss, rs, ls,
):
    y, x, zl, zh, c = (lax.axis_index(a) for a in AXES)
    t = zh * 2 + c
    s = (y * 4 + x) * 4 + zl

    loads = []
    pairs = [(w_hbm, w_ref), (k_hbm, k_ref), (v_hbm, v_ref), (taps_hbm, taps_ref)]
    pairs += [(fa_hbm, fa_ref), (ia_hbm, ia_ref), (q_hbm, q_ref), (cot_hbm, cot_ref)]
    for i, (src, dst) in enumerate(pairs):
        cp = pltpu.make_async_copy(src, dst, ls.at[1 + i])
        cp.start()
        loads.append(cp)

    def shift(v, d):
        return lax.rem(v + (d % 4), 4)

    def zxor(j):
        lo, hi = lax.rem(zl, 2), zl // 2
        lo = 1 - lo if j & 1 else lo
        hi = 1 - hi if j & 2 else hi
        return hi * 2 + lo

    def at_x(d):
        return (y, shift(x, d), zl, zh, c)

    def at_y(d):
        return (shift(y, d), x, zl, zh, c)

    def at_z(j):
        return (y, x, zxor(j), zh, c)

    def at_xz(d, j):
        return (y, shift(x, d), zxor(j), zh, c)

    def at_s(d):
        p = lax.rem(s + (d % 64), 64)
        return (p // 16, lax.rem(p // 4, 4), lax.rem(p, 4), zh, c)

    sibling = (y, x, zl, zh, 1 - c)
    across = (y, x, zl, 1 - zh, c)
    diagonal = (y, x, zl, 1 - zh, 1 - c)

    barrier = pltpu.get_barrier_semaphore()
    partners = [across, diagonal, at_s(1), at_s(63), at_z(3), at_z(2), at_z(1), at_x(2), at_y(2)]
    partners += [at_x(1), at_x(3), at_y(1), at_y(3), sibling]
    partners += [at_xz(d, j) for d in range(1, 4) for j in range(1, 4)]
    for dev in partners:
        pl.semaphore_signal(barrier, inc=1, device_id=dev, device_id_type=MESH)

    keys_of = {}
    sends = []

    def make(key, src, dst, dev):
        i = keys_of.setdefault(key, len(keys_of))
        return pltpu.make_async_remote_copy(
            src_ref=src,
            dst_ref=dst,
            send_sem=ss.at[i],
            recv_sem=rs.at[i],
            device_id=dev,
            device_id_type=MESH,
        )

    def send(key, src, dst, dev):
        cp = make(key, src, dst, dev)
        cp.start()
        sends.append(cp)

    def recv(key, dst, dev):
        make(key, dst, dst, dev).wait_recv()

    for cp in loads[:3]:
        cp.wait()
    own_w = pltpu.make_async_copy(
        w_ref, wbuf.at[pl.ds(pl.multiple_of(s * 64, 64), 64)], ls.at[0]
    )
    own_w.start()
    for i in range(4):
        cols = pl.ds(i * 256, 256)
        prod[:, cols] = (k_ref[:, cols].astype(F32) * v_ref[:, cols].astype(F32)).astype(BF16)

    def chunk(j, a, b, part=None):
        dx, dy = (a, b) if j % 2 == 0 else (b, a)
        off = ((shift(y, dy) * 4 + shift(x, dx)) * 4 + zxor(j)) * 64
        size = 64
        if part is not None:
            off, size = off + 32 * part, 32
        return wbuf.at[pl.ds(pl.multiple_of(off, size), size)]

    def step(j, first, d):
        along_x = (j % 2 == 0) == first
        return at_x(d) if along_x else at_y(d)

    def source(j, a):
        return w_ref if j == 0 and a == 0 else chunk(j, a, 0)

    def second(j, a):
        src = source(j, a)
        send(("u1", j, a), src, chunk(j, a, 0), step(j, False, 1))
        send(("u2", j, a), src, chunk(j, a, 0), step(j, False, -1))

    def s1(j):
        src = source(j, 0)
        send(("t1", j), src, chunk(j, 0, 0), step(j, True, 1))
        send(("t2", j), src, chunk(j, 0, 0), step(j, True, -1))
        second(j, 0)

    def s2_(j):
        recv(("t1", j), chunk(j, -1, 0), step(j, True, 1))
        send(("t3", j), chunk(j, -1, 0, 0), chunk(j, -1, 0, 0), step(j, True, 1))
        recv(("t2", j), chunk(j, 1, 0), step(j, True, -1))
        send(("t4", j), chunk(j, 1, 0, 1), chunk(j, 1, 0, 1), step(j, True, -1))
        second(j, -1)
        second(j, 1)

    def s3_(j):
        recv(("t3", j), chunk(j, 2, 0, 0), step(j, True, 1))
        recv(("t4", j), chunk(j, 2, 0, 1), step(j, True, -1))
        second(j, 2)

    def relay(j, a):
        recv(("u1", j, a), chunk(j, a, -1), step(j, False, 1))
        send(("u3", j, a), chunk(j, a, -1, 0), chunk(j, a, -1, 0), step(j, False, 1))
        recv(("u2", j, a), chunk(j, a, 1), step(j, False, -1))
        send(("u4", j, a), chunk(j, a, 1, 1), chunk(j, a, 1, 1), step(j, False, -1))

    def last(j, a):
        recv(("u3", j, a), chunk(j, a, 2, 0), step(j, False, 1))
        recv(("u4", j, a), chunk(j, a, 2, 1), step(j, False, -1))

    def own_place(j):
        return wbuf.at[pl.ds(pl.multiple_of(((y * 4 + x) * 4 + zxor(j)) * 64, 64), 64)]

    def half_of(p):
        return zl // 2 if p == 0 else 1 - zl // 2

    def gg_copy(p, dy):
        yy, h = shift(y, dy), half_of(p)
        delta = lax.rem(yy + 4 - t, 4)
        i = gg_base + p * 4 + delta
        return delta, pltpu.make_async_remote_copy(
            src_ref=ggs.at[yy, h],
            dst_ref=ggr.at[delta],
            send_sem=ss.at[i],
            recv_sem=rs.at[i],
            device_id=(y, x, zl, yy // 2, lax.rem(yy, 2)),
            device_id_type=MESH,
        )

    def batch(p, dy):
        yy, h = shift(y, dy), half_of(p)

        def one(i, carry):
            rows = pl.ds(pl.multiple_of(yy * 1024 + i * 256 + h * 128, 128), 128)
            part = dot(cot_ref[...], wbuf[rows, :], ((1,), (1,)))
            ggs[yy, h, i] = part.astype(BF16)
            return carry

        lax.fori_loop(0, 4, one, 0, unroll=True)
        if p == 1:
            delta, cp = gg_copy(p, dy)

            @pl.when(delta != 0)
            def _():
                cp.start()

    gg_base = 160
    halo_base = 168

    row = lax.broadcasted_iota(jnp.int32, (2 * LEN, 128), 0)
    sign = (1 - 2 * lax.rem(row, 2)).astype(F32)
    inner = lax.broadcasted_iota(jnp.int32, (LEN, 128), 0) != 0

    def dft(val):
        return dot(fa_ref[0], val) + dot(fa_ref[1], val)

    def idft(val):
        hi = val.astype(BF16)
        lo = (val - hi.astype(F32)).astype(BF16)
        return dot(ia_ref[0], hi) + dot(ia_ref[0], lo) + dot(ia_ref[1], hi)

    def cmul(a, b, conj):
        ar, ai, br, bi = a[:LEN], a[LEN:], b[:LEN], b[LEN:]
        ii = ai * bi
        if conj:
            re = ar * br + jnp.where(inner, ii, 0.0)
            im = jnp.where(inner, ai * br - ar * bi, ii)
        else:
            re = ar * br - jnp.where(inner, ii, 0.0)
            im = jnp.where(inner, ai * br + ar * bi, ii)
        return jnp.concatenate([re, im], 0)

    def strips(fn):
        def one(e, carry):
            fn(e, pl.ds(pl.multiple_of(e * 128, 128), 128))
            return carry

        lax.fori_loop(0, 8, one, 0, unroll=True)

    here = seg_ref[s]
    back = seg_ref[jnp.maximum(s - 1, 0)]
    ahead = seg_ref[jnp.minimum(s + 1, 63)]
    linked = jnp.where(jnp.logical_and(s > 0, here == back), 1.0, 0.0).astype(F32)
    linked_next = jnp.where(jnp.logical_and(s < 63, here == ahead), 1.0, 0.0).astype(F32)

    def rows_of(place, size):
        return pl.ds(pl.multiple_of(place * size, size), size)

    def half_copy(base, h, src, dst, dev):
        return pltpu.make_async_remote_copy(
            src_ref=src,
            dst_ref=dst,
            send_sem=ss.at[base + h],
            recv_sem=rs.at[base + h],
            device_id=dev,
            device_id_type=MESH,
        )

    def half_tail(p):
        h = half_of(p)
        if p == 0:
            recv("k1", gs0, sibling)
            recv("k3", ga0, across)
        else:
            for delta in range(1, 4):
                i = gg_base + p * 4 + delta
                pltpu.make_async_remote_copy(
                    src_ref=ggr.at[delta],
                    dst_ref=ggr.at[delta],
                    send_sem=ss.at[i],
                    recv_sem=rs.at[i],
                    device_id=sibling,
                    device_id_type=MESH,
                ).wait_recv()

        def cols_of(i):
            return pl.ds(pl.multiple_of(i * 256 + h * 128, 128), 128)

        def gradients(i, carry):
            cols = cols_of(i)
            total = ggs[t, h, i].astype(F32)
            if p == 0:
                total = total + gs0[i].astype(F32) + ga0[i].astype(F32)
            else:
                for delta in range(1, 4):
                    total = total + ggr[delta, i].astype(F32)
            gg = total.astype(BF16).astype(F32)
            gfb[h, i] = (gg * q_ref[:, cols].astype(F32)).astype(BF16)
            gq_ref[:, cols] = (gg * fil[:, cols].astype(F32)).astype(BF16)
            return carry

        lax.fori_loop(0, 4, gradients, 0, unroll=True)
        half_copy(halo_base, h, gfb.at[h], gnx.at[h], at_s(-1)).start()

        def taps_part(i, carry):
            cols = cols_of(i)
            spec = dft(gfb[h, i])
            e = i * 2 + h
            gft[e] = spec
            part = idft(cmul(spec, xbuf[e], True)).T
            tgf[cols, :] = part
            tgs[cols, :] = part.astype(BF16)
            return carry

        lax.fori_loop(0, 4, taps_part, 0, unroll=True)
        for d in (2, 1, 3):
            rows = pl.ds(pl.multiple_of(shift(y, d) * 256 + h * 128, 128), 128)
            here = pl.ds(pl.multiple_of(h * 128, 128), 128)
            send(("r1", p, d), tgs.at[rows], r1.at[d - 1, here], at_y(d))

    def r1_rows(p):
        return pl.ds(pl.multiple_of(half_of(p) * 128, 128), 128)

    def backward(h):
        half_copy(halo_base, h, gfb.at[h], gnx.at[h], at_s(-1)).wait_recv()

        def one(i, carry):
            e = i * 2 + h
            cols = pl.ds(pl.multiple_of(e * 128, 128), 128)
            spec = gft[e] + linked_next * (sign * dft(gnx[h, i]))
            gp = idft(cmul(spec, tbuf[e], True)).astype(BF16).astype(F32)
            gk_ref[:, cols] = (gp * v_ref[:, cols].astype(F32)).astype(BF16)
            gv_ref[:, cols] = (gp * k_ref[:, cols].astype(F32)).astype(BF16)
            return carry

        lax.fori_loop(0, 4, one, 0, unroll=True)

    for cp in loads[3:]:
        cp.wait()
    pl.semaphore_wait(barrier, len(partners))

    s1(0)
    send("z1", w_ref, own_place(0), at_z(1))
    send("z2", w_ref, own_place(0), at_z(2))
    send("halo", prod, prev, at_s(1))

    def spectra(e, cols):
        tap = taps_ref[cols, :]
        tbuf[e] = dot(fa_ref[0], tap, ((1,), (1,))) + dot(fa_ref[1], tap, ((1,), (1,)))
        xbuf[e] = dft(prod[:, cols])

    strips(spectra)
    own_w.wait()

    recv("z1", own_place(1), at_z(1))
    send("z3", own_place(1), own_place(1), at_z(2))
    s1(1)
    s2_(0)
    s2_(1)
    s3_(0)
    s3_(1)
    relay(0, 0)
    relay(1, 0)
    recv("z2", own_place(2), at_z(2))
    s1(2)
    recv("halo", prev, at_s(1))

    def forward(e, cols):
        spec = xbuf[e] + linked * (sign * dft(prev[:, cols]))
        xbuf[e] = spec
        filt = idft(cmul(spec, tbuf[e], False)).astype(BF16)
        fil[:, cols] = filt
        gbuf[t, :, cols] = (q_ref[:, cols].astype(F32) * filt.astype(F32)).astype(BF16)

    strips(forward)
    t_sib, t_acr, t_dia = zh * 2 + 1 - c, (1 - zh) * 2 + c, (1 - zh) * 2 + 1 - c
    send("g2", gbuf.at[t], gbuf.at[t], across)
    send("g1", gbuf.at[t], gbuf.at[t], sibling)

    relay(0, -1)
    relay(1, -1)
    relay(0, 1)
    relay(1, 1)
    recv("z3", own_place(3), at_z(2))
    s1(3)
    s2_(2)
    relay(0, 2)
    relay(1, 2)
    s2_(3)
    last(0, 0)
    last(1, 0)
    batch(0, 0)
    s3_(2)
    s3_(3)
    relay(2, 0)
    relay(3, 0)
    for a in (-1, 1):
        last(0, a)
        last(1, a)
    last(0, 2)
    batch(0, -1)
    relay(2, -1)
    relay(3, -1)
    batch(0, 1)
    relay(2, 1)
    relay(3, 1)
    last(1, 2)
    batch(0, 2)
    first = half_of(0)
    send("k2", ggs.at[t_dia, first], x0, sibling)
    send("k1", ggs.at[t_sib, first], gs0, sibling)
    relay(2, 2)
    relay(3, 2)
    recv("k2", x0, sibling)
    xs[...] = (ggs[t_acr, first].astype(F32) + x0[...].astype(F32)).astype(BF16)
    send("k3", xs, ga0, across)
    last(2, 0)
    last(3, 0)
    batch(1, 0)
    for a in (-1, 1):
        last(2, a)
        last(3, a)
    last(2, 2)
    batch(1, -1)
    batch(1, 1)
    last(3, 2)
    batch(1, 2)

    half_tail(0)
    recv("g2", gbuf.at[t_acr], across)
    send("g3", gbuf.at[t_acr], gbuf.at[t_acr], sibling)
    half_tail(1)

    @pl.when(lax.rem(zl, 2) == 0)
    def _():
        backward(half_of(0))

    def outputs(n):
        cols = pl.ds(n * 256, 256)
        total = dot(gbuf[0], wbuf[0:1024, cols])
        for i in range(1, 4):
            total = total + dot(gbuf[i], wbuf[i * 1024 : (i + 1) * 1024, cols])
        out_ref[:, cols] = total.astype(BF16)

    for p in range(2):
        for d in range(1, 4):
            recv(("r1", p, d), r1.at[d - 1, r1_rows(p)], at_y(d))
    total = tgf[rows_of(y, 256), :]
    for d in range(3):
        total = total + r1[d].astype(F32)
    s2[...] = total
    for d in (2, 1, 3, 0):
        for j in (3, 2, 1, 0):
            if d or j:
                rows = rows_of(shift(x, d) * 4 + zxor(j), 16)
                send(("r2", d, j), s2.at[rows], r2.at[d * 4 + j], at_xz(d, j))

    recv("g1", gbuf.at[t_sib], sibling)
    recv("g3", gbuf.at[t_dia], sibling)
    for n in range(4):
        outputs(n)
    backward(half_of(1))

    @pl.when(lax.rem(zl, 2) == 1)
    def _():
        backward(half_of(0))

    total = s2[rows_of(x * 4 + zl, 16), :]
    for d in range(4):
        for j in range(4):
            if d or j:
                recv(("r2", d, j), r2.at[d * 4 + j], at_xz(d, j))
                total = total + r2[d * 4 + j]
    tg_ref[...] = total

    for h in range(2):
        half_copy(halo_base, h, gfb.at[h], gnx.at[h], at_s(-1)).wait_send()
    for cp in sends:
        cp.wait_send()
    for dy in (0, -1, 1, 2):
        delta, cp = gg_copy(1, dy)

        @pl.when(delta != 0)
        def _(cp=cp):
            cp.wait_send()

    assert len(keys_of) <= gg_base


def write_out(*refs):
    ins, outs, bufs, sem = refs[:5], refs[5:10], refs[10:15], refs[15]
    reads = [pltpu.make_async_copy(ins[i], bufs[i], sem.at[i]) for i in range(5)]
    writes = [pltpu.make_async_copy(bufs[i], outs[i], sem.at[5 + i]) for i in range(5)]
    for cp in reads:
        cp.start()
    for read, write in zip(reads, writes):
        read.wait()
        write.start()
    for cp in writes:
        cp.wait()


def on_device(queries, keys, values, w_out, taps, seg_ids, cotangent):
    fwd, inv = dft_tables()
    block = queries.shape
    vmem = pl.BlockSpec(memory_space=pltpu.VMEM)
    hbm = pl.BlockSpec(memory_space=pl.ANY)
    smem = pl.BlockSpec(memory_space=pltpu.SMEM)
    outs = [jax.ShapeDtypeStruct(block, BF16)] * 4 + [jax.ShapeDtypeStruct((16, LEN), F32)]
    scratch = [
        pltpu.VMEM(block, BF16),
        pltpu.VMEM(block, BF16),
        pltpu.VMEM(block, BF16),
        pltpu.VMEM((64, 1024), BF16),
        pltpu.VMEM((1024, LEN), BF16),
        pltpu.VMEM(block, BF16),
        pltpu.VMEM((2, 256, 128), BF16),
        pltpu.VMEM((2, 128, 256), BF16),
        pltpu.VMEM((4096, 1024), BF16),
        pltpu.VMEM(block, BF16),
        pltpu.VMEM(block, BF16),
        pltpu.VMEM((8, 256, 128), F32),
        pltpu.VMEM((8, 256, 128), F32),
        pltpu.VMEM(block, BF16),
        pltpu.VMEM((4, *block), BF16),
        pltpu.VMEM((4, 2, 4, 128, 128), BF16),
        pltpu.VMEM((4, 4, 128, 128), BF16),
        pltpu.VMEM((4, 128, 128), BF16),
        pltpu.VMEM((4, 128, 128), BF16),
        pltpu.VMEM((4, 128, 128), BF16),
        pltpu.VMEM((4, 128, 128), BF16),
        pltpu.VMEM((2, 4, 128, 128), BF16),
        pltpu.VMEM((2, 4, 128, 128), BF16),
        pltpu.VMEM((8, 256, 128), F32),
        pltpu.VMEM((1024, LEN), F32),
        pltpu.VMEM((1024, LEN), BF16),
        pltpu.VMEM((3, 256, LEN), BF16),
        pltpu.VMEM((256, LEN), F32),
        pltpu.VMEM((16, 16, LEN), F32),
        pltpu.SemaphoreType.DMA((170,)),
        pltpu.SemaphoreType.DMA((170,)),
        pltpu.SemaphoreType.DMA((9,)),
    ]
    results = pl.pallas_call(
        kernel,
        out_shape=outs,
        in_specs=[hbm] * 5 + [smem] + [hbm] * 3,
        out_specs=[vmem] * 5,
        scratch_shapes=scratch,
        compiler_params=pltpu.CompilerParams(
            collective_id=0, has_side_effects=True, vmem_limit_bytes=67043328
        ),
        name="hyena",
    )(queries, keys, values, w_out, taps, seg_ids, cotangent, jnp.asarray(fwd), jnp.asarray(inv))
    return pl.pallas_call(
        write_out,
        out_shape=outs,
        in_specs=[hbm] * 5,
        out_specs=[hbm] * 5,
        scratch_shapes=[pltpu.VMEM(o.shape, o.dtype) for o in outs]
        + [pltpu.SemaphoreType.DMA((10,))],
        compiler_params=pltpu.CompilerParams(vmem_limit_bytes=67043328),
        name="write_out",
    )(*results)


def solution(mesh):
    split = Mesh(mesh.devices.reshape(4, 4, 4, 2, 2), AXES)
    rows = P(SEQ, TP)
    in_specs = (rows, rows, rows, rows, P(TP, None), P(), rows)
    out_specs = (rows, rows, rows, rows, P(TP + SEQ, None))
    return jax.shard_map(
        on_device, mesh=split, in_specs=in_specs, out_specs=out_specs, check_vma=False
    )
```

```python
import functools

import jax
import jax.numpy as jnp
import numpy as np
from jax import lax
from jax.experimental import pallas as pl
from jax.experimental.pallas import tpu as pltpu
from jax.sharding import Mesh
from jax.sharding import PartitionSpec as P

AXES = ("y", "x", "zl", "zh", "c")
SEQ = ("y", "x", "zl")
TP = ("zh", "c")
LEN = 128
MESH = pl.DeviceIdType.MESH
F32 = jnp.float32
BF16 = jnp.bfloat16


def split_hi_lo(mat):
    hi = np.asarray(mat, np.float32).astype(jnp.bfloat16)
    lo = (mat - hi.astype(np.float64)).astype(np.float32).astype(jnp.bfloat16)
    return np.stack([hi, lo])


def dft_tables():
    n = np.arange(LEN)
    ang = 2 * np.pi * np.outer(n, n) / (2 * LEN)
    alt = np.where(n % 2 == 0, 1.0, -1.0)
    fwd = np.concatenate([np.cos(ang), -np.sin(ang)], 0)
    fwd[LEN] = alt
    inv = np.concatenate([np.cos(ang), -np.sin(ang)], 1) / LEN
    inv[:, 0] = 0.5 / LEN
    inv[:, LEN] = alt * (0.5 / LEN)
    return split_hi_lo(fwd), split_hi_lo(inv)


def dot(a, b, dims=((1,), (0,))):
    return lax.dot_general(a, b, (dims, ((), ())), preferred_element_type=F32)


def kernel(
    q_hbm, k_hbm, v_hbm, w_hbm, taps_hbm, seg_ref, cot_hbm, fa_hbm, ia_hbm,
    out_ref, gq_ref, gk_ref, gv_ref, tg_ref,
    q_ref, k_ref, v_ref, w_ref, taps_ref, cot_ref, fa_ref, ia_ref,
    wbuf, prod, prev, tbuf, xbuf, fil, gbuf, ggs, gs0, ga0, x0, xs, gfb, gnx, gft,
    tgf, tgs, r1, s2, r2, ss, rs, ls,
):
    y, x, zl, zh, c = (lax.axis_index(a) for a in AXES)
    t = zh * 2 + c
    s = (y * 4 + x) * 4 + zl

    loads = []
    pairs = [(w_hbm, w_ref), (k_hbm, k_ref), (v_hbm, v_ref), (taps_hbm, taps_ref)]
    pairs += [(fa_hbm, fa_ref), (ia_hbm, ia_ref), (q_hbm, q_ref), (cot_hbm, cot_ref)]
    for i, (src, dst) in enumerate(pairs):
        cp = pltpu.make_async_copy(src, dst, ls.at[1 + i])
        cp.start()
        loads.append(cp)

    def shift(v, d):
        return lax.rem(v + (d % 4), 4)

    def zxor(j):
        lo, hi = lax.rem(zl, 2), zl // 2
        lo = 1 - lo if j & 1 else lo
        hi = 1 - hi if j & 2 else hi
        return hi * 2 + lo

    def at_x(d):
        return (y, shift(x, d), zl, zh, c)

    def at_y(d):
        return (shift(y, d), x, zl, zh, c)

    def at_z(j):
        return (y, x, zxor(j), zh, c)

    def at_xz(d, j):
        return (y, shift(x, d), zxor(j), zh, c)

    def at_s(d):
        p = lax.rem(s + (d % 64), 64)
        return (p // 16, lax.rem(p // 4, 4), lax.rem(p, 4), zh, c)

    sibling = (y, x, zl, zh, 1 - c)
    across = (y, x, zl, 1 - zh, c)
    diagonal = (y, x, zl, 1 - zh, 1 - c)

    barrier = pltpu.get_barrier_semaphore()
    partners = [across, diagonal, at_s(1), at_s(63), at_z(3), at_z(2), at_z(1), at_x(2), at_y(2)]
    partners += [at_x(1), at_x(3), at_y(1), at_y(3), sibling]
    partners += [at_xz(d, j) for d in range(1, 4) for j in range(1, 4)]
    for dev in partners:
        pl.semaphore_signal(barrier, inc=1, device_id=dev, device_id_type=MESH)

    keys_of = {}
    sends = []

    def make(key, src, dst, dev):
        i = keys_of.setdefault(key, len(keys_of))
        return pltpu.make_async_remote_copy(
            src_ref=src,
            dst_ref=dst,
            send_sem=ss.at[i],
            recv_sem=rs.at[i],
            device_id=dev,
            device_id_type=MESH,
        )

    def send(key, src, dst, dev):
        cp = make(key, src, dst, dev)
        cp.start()
        sends.append(cp)

    def recv(key, dst, dev):
        make(key, dst, dst, dev).wait_recv()

    for cp in loads[:3]:
        cp.wait()
    own_w = pltpu.make_async_copy(
        w_ref, wbuf.at[pl.ds(pl.multiple_of(s * 64, 64), 64)], ls.at[0]
    )
    own_w.start()
    for i in range(4):
        cols = pl.ds(i * 256, 256)
        prod[:, cols] = (k_ref[:, cols].astype(F32) * v_ref[:, cols].astype(F32)).astype(BF16)

    def chunk(j, a, b, part=None):
        dx, dy = (a, b) if j % 2 == 0 else (b, a)
        off = ((shift(y, dy) * 4 + shift(x, dx)) * 4 + zxor(j)) * 64
        size = 64
        if part is not None:
            off, size = off + 32 * part, 32
        return wbuf.at[pl.ds(pl.multiple_of(off, size), size)]

    def step(j, first, d):
        along_x = (j % 2 == 0) == first
        return at_x(d) if along_x else at_y(d)

    def source(j, a):
        return w_ref if j == 0 and a == 0 else chunk(j, a, 0)

    def second(j, a):
        src = source(j, a)
        send(("u1", j, a), src, chunk(j, a, 0), step(j, False, 1))
        send(("u2", j, a), src, chunk(j, a, 0), step(j, False, -1))

    def s1(j):
        src = source(j, 0)
        send(("t1", j), src, chunk(j, 0, 0), step(j, True, 1))
        send(("t2", j), src, chunk(j, 0, 0), step(j, True, -1))
        second(j, 0)

    def s2_(j):
        recv(("t1", j), chunk(j, -1, 0), step(j, True, 1))
        send(("t3", j), chunk(j, -1, 0, 0), chunk(j, -1, 0, 0), step(j, True, 1))
        recv(("t2", j), chunk(j, 1, 0), step(j, True, -1))
        send(("t4", j), chunk(j, 1, 0, 1), chunk(j, 1, 0, 1), step(j, True, -1))
        second(j, -1)
        second(j, 1)

    def s3_(j):
        recv(("t3", j), chunk(j, 2, 0, 0), step(j, True, 1))
        recv(("t4", j), chunk(j, 2, 0, 1), step(j, True, -1))
        second(j, 2)

    def relay(j, a):
        recv(("u1", j, a), chunk(j, a, -1), step(j, False, 1))
        send(("u3", j, a), chunk(j, a, -1, 0), chunk(j, a, -1, 0), step(j, False, 1))
        recv(("u2", j, a), chunk(j, a, 1), step(j, False, -1))
        send(("u4", j, a), chunk(j, a, 1, 1), chunk(j, a, 1, 1), step(j, False, -1))

    def last(j, a):
        recv(("u3", j, a), chunk(j, a, 2, 0), step(j, False, 1))
        recv(("u4", j, a), chunk(j, a, 2, 1), step(j, False, -1))

    def own_place(j):
        return wbuf.at[pl.ds(pl.multiple_of(((y * 4 + x) * 4 + zxor(j)) * 64, 64), 64)]

    def half_of(p):
        return zl // 2 if p == 0 else 1 - zl // 2

    t_sib, t_acr, t_dia = zh * 2 + 1 - c, (1 - zh) * 2 + c, (1 - zh) * 2 + 1 - c
    to_sum = make("k2b", ggs.at[t_dia, half_of(1)], x0.at[1], sibling)
    to_sibling = make("k1b", ggs.at[t_sib, half_of(1)], gs0.at[1], sibling)
    to_far = make("k3b", xs.at[1], ga0.at[1], across)

    def batch(p, dy):
        yy, h = shift(y, dy), half_of(p)

        def one(i, carry):
            rows = pl.ds(pl.multiple_of(yy * 1024 + i * 256 + h * 128, 128), 128)
            part = dot(cot_ref[...], wbuf[rows, :], ((1,), (1,)))
            ggs[yy, h, i] = part.astype(BF16)
            return carry

        lax.fori_loop(0, 4, one, 0, unroll=True)
        if p == 1:

            @pl.when(yy == t_dia)
            def _():
                to_sum.start()

            @pl.when(yy == t_sib)
            def _():
                to_sibling.start()

    def far_share(dy):
        @pl.when(shift(y, dy) == t_acr)
        def _():
            to_sum.wait_recv()
            xs[1] = (ggs[t_acr, half_of(1)].astype(F32) + x0[1].astype(F32)).astype(BF16)
            to_far.start()

    gg_base = 160
    halo_base = 168

    row = lax.broadcasted_iota(jnp.int32, (2 * LEN, 128), 0)
    sign = (1 - 2 * lax.rem(row, 2)).astype(F32)
    inner = lax.broadcasted_iota(jnp.int32, (LEN, 128), 0) != 0

    def dft(val):
        return dot(fa_ref[0], val) + dot(fa_ref[1], val)

    def idft(val):
        hi = val.astype(BF16)
        lo = (val - hi.astype(F32)).astype(BF16)
        return dot(ia_ref[0], hi) + dot(ia_ref[0], lo) + dot(ia_ref[1], hi)

    def cmul(a, b, conj):
        ar, ai, br, bi = a[:LEN], a[LEN:], b[:LEN], b[LEN:]
        ii = ai * bi
        if conj:
            re = ar * br + jnp.where(inner, ii, 0.0)
            im = jnp.where(inner, ai * br - ar * bi, ii)
        else:
            re = ar * br - jnp.where(inner, ii, 0.0)
            im = jnp.where(inner, ai * br + ar * bi, ii)
        return jnp.concatenate([re, im], 0)

    def strips(fn):
        def one(e, carry):
            fn(e, pl.ds(pl.multiple_of(e * 128, 128), 128))
            return carry

        lax.fori_loop(0, 8, one, 0, unroll=True)

    here = seg_ref[s]
    back = seg_ref[jnp.maximum(s - 1, 0)]
    ahead = seg_ref[jnp.minimum(s + 1, 63)]
    linked = jnp.where(jnp.logical_and(s > 0, here == back), 1.0, 0.0).astype(F32)
    linked_next = jnp.where(jnp.logical_and(s < 63, here == ahead), 1.0, 0.0).astype(F32)

    def rows_of(place, size):
        return pl.ds(pl.multiple_of(place * size, size), size)

    def half_copy(base, h, src, dst, dev):
        return pltpu.make_async_remote_copy(
            src_ref=src,
            dst_ref=dst,
            send_sem=ss.at[base + h],
            recv_sem=rs.at[base + h],
            device_id=dev,
            device_id_type=MESH,
        )

    def half_tail(p):
        h = half_of(p)
        if p == 0:
            recv("k1", gs0.at[0], sibling)
            recv("k3", ga0.at[0], across)
        else:
            to_sibling.wait_recv()
            to_far.wait_recv()

        def cols_of(i):
            return pl.ds(pl.multiple_of(i * 256 + h * 128, 128), 128)

        def gradients(i, carry):
            cols = cols_of(i)
            total = ggs[t, h, i].astype(F32)
            total = total + gs0[p, i].astype(F32) + ga0[p, i].astype(F32)
            gg = total.astype(BF16).astype(F32)
            gfb[h, i] = (gg * q_ref[:, cols].astype(F32)).astype(BF16)
            gq_ref[:, cols] = (gg * fil[:, cols].astype(F32)).astype(BF16)
            return carry

        lax.fori_loop(0, 4, gradients, 0, unroll=True)
        half_copy(halo_base, h, gfb.at[h], gnx.at[h], at_s(-1)).start()

        def taps_part(i, carry):
            cols = cols_of(i)
            spec = dft(gfb[h, i])
            e = i * 2 + h
            gft[e] = spec
            part = idft(cmul(spec, xbuf[e], True)).T
            tgf[cols, :] = part
            tgs[cols, :] = part.astype(BF16)
            return carry

        lax.fori_loop(0, 4, taps_part, 0, unroll=True)
        for d in (2, 1, 3):
            rows = pl.ds(pl.multiple_of(shift(y, d) * 256 + h * 128, 128), 128)
            here = pl.ds(pl.multiple_of(h * 128, 128), 128)
            send(("r1", p, d), tgs.at[rows], r1.at[d - 1, here], at_y(d))

    def r1_rows(p):
        return pl.ds(pl.multiple_of(half_of(p) * 128, 128), 128)

    def backward(h):
        half_copy(halo_base, h, gfb.at[h], gnx.at[h], at_s(-1)).wait_recv()

        def one(i, carry):
            e = i * 2 + h
            cols = pl.ds(pl.multiple_of(e * 128, 128), 128)
            spec = gft[e] + linked_next * (sign * dft(gnx[h, i]))
            gp = idft(cmul(spec, tbuf[e], True)).astype(BF16).astype(F32)
            gk_ref[:, cols] = (gp * v_ref[:, cols].astype(F32)).astype(BF16)
            gv_ref[:, cols] = (gp * k_ref[:, cols].astype(F32)).astype(BF16)
            return carry

        lax.fori_loop(0, 4, one, 0, unroll=True)

    for cp in loads[3:]:
        cp.wait()
    pl.semaphore_wait(barrier, len(partners))

    s1(0)
    send("z1", w_ref, own_place(0), at_z(1))
    send("z2", w_ref, own_place(0), at_z(2))
    send("halo", prod, prev, at_s(1))

    def spectra(e, cols):
        tap = taps_ref[cols, :]
        tbuf[e] = dot(fa_ref[0], tap, ((1,), (1,))) + dot(fa_ref[1], tap, ((1,), (1,)))
        xbuf[e] = dft(prod[:, cols])

    strips(spectra)
    own_w.wait()

    recv("z1", own_place(1), at_z(1))
    send("z3", own_place(1), own_place(1), at_z(2))
    s1(1)
    s2_(0)
    s2_(1)
    s3_(0)
    s3_(1)
    relay(0, 0)
    relay(1, 0)
    recv("z2", own_place(2), at_z(2))
    s1(2)
    recv("halo", prev, at_s(1))

    def forward(e, cols):
        spec = xbuf[e] + linked * (sign * dft(prev[:, cols]))
        xbuf[e] = spec
        filt = idft(cmul(spec, tbuf[e], False)).astype(BF16)
        fil[:, cols] = filt
        gbuf[t, :, cols] = (q_ref[:, cols].astype(F32) * filt.astype(F32)).astype(BF16)

    strips(forward)
    send("g2", gbuf.at[t], gbuf.at[t], across)
    send("g1", gbuf.at[t], gbuf.at[t], sibling)

    relay(0, -1)
    relay(1, -1)
    relay(0, 1)
    relay(1, 1)
    recv("z3", own_place(3), at_z(2))
    s1(3)
    s2_(2)
    relay(0, 2)
    relay(1, 2)
    s2_(3)
    last(0, 0)
    last(1, 0)
    batch(0, 0)
    s3_(2)
    s3_(3)
    relay(2, 0)
    relay(3, 0)
    for a in (-1, 1):
        last(0, a)
        last(1, a)
    last(0, 2)
    batch(0, -1)
    relay(2, -1)
    relay(3, -1)
    batch(0, 1)
    relay(2, 1)
    relay(3, 1)
    last(1, 2)
    batch(0, 2)
    first = half_of(0)
    send("k2", ggs.at[t_dia, first], x0.at[0], sibling)
    send("k1", ggs.at[t_sib, first], gs0.at[0], sibling)
    relay(2, 2)
    relay(3, 2)
    recv("k2", x0.at[0], sibling)
    xs[0] = (ggs[t_acr, first].astype(F32) + x0[0].astype(F32)).astype(BF16)
    send("k3", xs.at[0], ga0.at[0], across)
    last(2, 0)
    last(3, 0)
    batch(1, 0)
    for a in (-1, 1):
        last(2, a)
        last(3, a)
    last(2, 2)
    batch(1, -1)
    far_share(0)
    batch(1, 1)
    far_share(-1)
    last(3, 2)
    batch(1, 2)
    far_share(1)
    far_share(2)

    half_tail(0)
    recv("g2", gbuf.at[t_acr], across)
    send("g3", gbuf.at[t_acr], gbuf.at[t_acr], sibling)
    half_tail(1)

    @pl.when(lax.rem(zl, 2) == 0)
    def _():
        backward(half_of(0))

    def outputs(n):
        cols = pl.ds(n * 256, 256)
        total = dot(gbuf[0], wbuf[0:1024, cols])
        for i in range(1, 4):
            total = total + dot(gbuf[i], wbuf[i * 1024 : (i + 1) * 1024, cols])
        out_ref[:, cols] = total.astype(BF16)

    for p in range(2):
        for d in range(1, 4):
            recv(("r1", p, d), r1.at[d - 1, r1_rows(p)], at_y(d))
    total = tgf[rows_of(y, 256), :]
    for d in range(3):
        total = total + r1[d].astype(F32)
    s2[...] = total
    for d in (2, 1, 3, 0):
        for j in (3, 2, 1, 0):
            if d or j:
                rows = rows_of(shift(x, d) * 4 + zxor(j), 16)
                send(("r2", d, j), s2.at[rows], r2.at[d * 4 + j], at_xz(d, j))

    recv("g1", gbuf.at[t_sib], sibling)
    recv("g3", gbuf.at[t_dia], sibling)
    for n in range(4):
        outputs(n)
    backward(half_of(1))

    @pl.when(lax.rem(zl, 2) == 1)
    def _():
        backward(half_of(0))

    total = s2[rows_of(x * 4 + zl, 16), :]
    for d in range(4):
        for j in range(4):
            if d or j:
                recv(("r2", d, j), r2.at[d * 4 + j], at_xz(d, j))
                total = total + r2[d * 4 + j]
    tg_ref[...] = total

    for h in range(2):
        half_copy(halo_base, h, gfb.at[h], gnx.at[h], at_s(-1)).wait_send()
    for cp in sends:
        cp.wait_send()
    for cp in (to_sum, to_sibling, to_far):
        cp.wait_send()

    assert len(keys_of) <= gg_base


def write_out(*refs):
    ins, outs, bufs, sem = refs[:5], refs[5:10], refs[10:15], refs[15]
    reads = [pltpu.make_async_copy(ins[i], bufs[i], sem.at[i]) for i in range(5)]
    writes = [pltpu.make_async_copy(bufs[i], outs[i], sem.at[5 + i]) for i in range(5)]
    for cp in reads:
        cp.start()
    for read, write in zip(reads, writes):
        read.wait()
        write.start()
    for cp in writes:
        cp.wait()


def on_device(queries, keys, values, w_out, taps, seg_ids, cotangent):
    fwd, inv = dft_tables()
    block = queries.shape
    vmem = pl.BlockSpec(memory_space=pltpu.VMEM)
    hbm = pl.BlockSpec(memory_space=pl.ANY)
    smem = pl.BlockSpec(memory_space=pltpu.SMEM)
    outs = [jax.ShapeDtypeStruct(block, BF16)] * 4 + [jax.ShapeDtypeStruct((16, LEN), F32)]
    scratch = [
        pltpu.VMEM(block, BF16),
        pltpu.VMEM(block, BF16),
        pltpu.VMEM(block, BF16),
        pltpu.VMEM((64, 1024), BF16),
        pltpu.VMEM((1024, LEN), BF16),
        pltpu.VMEM(block, BF16),
        pltpu.VMEM((2, 256, 128), BF16),
        pltpu.VMEM((2, 128, 256), BF16),
        pltpu.VMEM((4096, 1024), BF16),
        pltpu.VMEM(block, BF16),
        pltpu.VMEM(block, BF16),
        pltpu.VMEM((8, 256, 128), F32),
        pltpu.VMEM((8, 256, 128), F32),
        pltpu.VMEM(block, BF16),
        pltpu.VMEM((4, *block), BF16),
        pltpu.VMEM((4, 2, 4, 128, 128), BF16),
        pltpu.VMEM((2, 4, 128, 128), BF16),
        pltpu.VMEM((2, 4, 128, 128), BF16),
        pltpu.VMEM((2, 4, 128, 128), BF16),
        pltpu.VMEM((2, 4, 128, 128), BF16),
        pltpu.VMEM((2, 4, 128, 128), BF16),
        pltpu.VMEM((2, 4, 128, 128), BF16),
        pltpu.VMEM((8, 256, 128), F32),
        pltpu.VMEM((1024, LEN), F32),
        pltpu.VMEM((1024, LEN), BF16),
        pltpu.VMEM((3, 256, LEN), BF16),
        pltpu.VMEM((256, LEN), F32),
        pltpu.VMEM((16, 16, LEN), F32),
        pltpu.SemaphoreType.DMA((170,)),
        pltpu.SemaphoreType.DMA((170,)),
        pltpu.SemaphoreType.DMA((9,)),
    ]
    results = pl.pallas_call(
        kernel,
        out_shape=outs,
        in_specs=[hbm] * 5 + [smem] + [hbm] * 3,
        out_specs=[vmem] * 5,
        scratch_shapes=scratch,
        compiler_params=pltpu.CompilerParams(
            collective_id=0, has_side_effects=True, vmem_limit_bytes=67043328
        ),
        name="hyena",
    )(queries, keys, values, w_out, taps, seg_ids, cotangent, jnp.asarray(fwd), jnp.asarray(inv))
    return pl.pallas_call(
        write_out,
        out_shape=outs,
        in_specs=[hbm] * 5,
        out_specs=[hbm] * 5,
        scratch_shapes=[pltpu.VMEM(o.shape, o.dtype) for o in outs]
        + [pltpu.SemaphoreType.DMA((10,))],
        compiler_params=pltpu.CompilerParams(vmem_limit_bytes=67043328),
        name="write_out",
    )(*results)


def solution(mesh):
    split = Mesh(mesh.devices.reshape(4, 4, 4, 2, 2), AXES)
    rows = P(SEQ, TP)
    in_specs = (rows, rows, rows, rows, P(TP, None), P(), rows)
    out_specs = (rows, rows, rows, rows, P(TP + SEQ, None))
    return jax.shard_map(
        on_device, mesh=split, in_specs=in_specs, out_specs=out_specs, check_vma=False
    )
```

```python
import functools

import jax
import jax.numpy as jnp
import numpy as np
from jax import lax
from jax.experimental import pallas as pl
from jax.experimental.pallas import tpu as pltpu
from jax.sharding import Mesh
from jax.sharding import PartitionSpec as P

AXES = ("y", "x", "zl", "zh", "c")
SEQ = ("y", "x", "zl")
TP = ("zh", "c")
LEN = 128
MESH = pl.DeviceIdType.MESH
F32 = jnp.float32
BF16 = jnp.bfloat16


def split_hi_lo(mat):
    hi = np.asarray(mat, np.float32).astype(jnp.bfloat16)
    lo = (mat - hi.astype(np.float64)).astype(np.float32).astype(jnp.bfloat16)
    return np.stack([hi, lo])


def dft_tables():
    n = np.arange(LEN)
    ang = 2 * np.pi * np.outer(n, n) / (2 * LEN)
    alt = np.where(n % 2 == 0, 1.0, -1.0)
    fwd = np.concatenate([np.cos(ang), -np.sin(ang)], 0)
    fwd[LEN] = alt
    inv = np.concatenate([np.cos(ang), -np.sin(ang)], 1) / LEN
    inv[:, 0] = 0.5 / LEN
    inv[:, LEN] = alt * (0.5 / LEN)
    return split_hi_lo(fwd), split_hi_lo(inv)


def dot(a, b, dims=((1,), (0,))):
    return lax.dot_general(a, b, (dims, ((), ())), preferred_element_type=F32)


def kernel(
    q_hbm, k_hbm, v_hbm, w_hbm, taps_hbm, seg_ref, cot_hbm, fa_hbm, ia_hbm,
    out_ref, gq_ref, gk_ref, gv_ref, tg_ref,
    q_ref, k_ref, v_ref, w_ref, taps_ref, cot_ref, fa_ref, ia_ref,
    wbuf, prod, prev, tbuf, xbuf, fil, gbuf, ggs, gs0, ga0, x0, xs, gfb, gnx, gft,
    tgf, tgs, r1, s2, r2, ss, rs, ls,
):
    y, x, zl, zh, c = (lax.axis_index(a) for a in AXES)
    t = zh * 2 + c
    s = (y * 4 + x) * 4 + zl

    loads = []
    pairs = [(w_hbm, w_ref), (k_hbm, k_ref), (v_hbm, v_ref), (taps_hbm, taps_ref)]
    pairs += [(fa_hbm, fa_ref), (ia_hbm, ia_ref), (q_hbm, q_ref), (cot_hbm, cot_ref)]
    for i, (src, dst) in enumerate(pairs):
        cp = pltpu.make_async_copy(src, dst, ls.at[1 + i])
        cp.start()
        loads.append(cp)

    def shift(v, d):
        return lax.rem(v + (d % 4), 4)

    def zxor(j):
        lo, hi = lax.rem(zl, 2), zl // 2
        lo = 1 - lo if j & 1 else lo
        hi = 1 - hi if j & 2 else hi
        return hi * 2 + lo

    def at_x(d):
        return (y, shift(x, d), zl, zh, c)

    def at_y(d):
        return (shift(y, d), x, zl, zh, c)

    def at_z(j):
        return (y, x, zxor(j), zh, c)

    def at_xz(d, j):
        return (y, shift(x, d), zxor(j), zh, c)

    def at_s(d):
        p = lax.rem(s + (d % 64), 64)
        return (p // 16, lax.rem(p // 4, 4), lax.rem(p, 4), zh, c)

    sibling = (y, x, zl, zh, 1 - c)
    across = (y, x, zl, 1 - zh, c)
    diagonal = (y, x, zl, 1 - zh, 1 - c)

    barrier = pltpu.get_barrier_semaphore()
    partners = [across, diagonal, at_s(1), at_s(63), at_z(3), at_z(2), at_z(1), at_x(2), at_y(2)]
    partners += [at_x(1), at_x(3), at_y(1), at_y(3), sibling]
    partners += [at_xz(d, j) for d in range(1, 4) for j in range(1, 4)]
    for dev in partners:
        pl.semaphore_signal(barrier, inc=1, device_id=dev, device_id_type=MESH)

    keys_of = {}
    sends = []

    def make(key, src, dst, dev):
        i = keys_of.setdefault(key, len(keys_of))
        return pltpu.make_async_remote_copy(
            src_ref=src,
            dst_ref=dst,
            send_sem=ss.at[i],
            recv_sem=rs.at[i],
            device_id=dev,
            device_id_type=MESH,
        )

    def send(key, src, dst, dev):
        cp = make(key, src, dst, dev)
        cp.start()
        sends.append(cp)

    def recv(key, dst, dev):
        make(key, dst, dst, dev).wait_recv()

    for cp in loads[:3]:
        cp.wait()
    own_w = pltpu.make_async_copy(
        w_ref, wbuf.at[pl.ds(pl.multiple_of(s * 64, 64), 64)], ls.at[0]
    )
    own_w.start()
    for i in range(4):
        cols = pl.ds(i * 256, 256)
        prod[:, cols] = (k_ref[:, cols].astype(F32) * v_ref[:, cols].astype(F32)).astype(BF16)

    def chunk(j, a, b, part=None):
        dx, dy = (a, b) if j % 2 == 0 else (b, a)
        off = ((shift(y, dy) * 4 + shift(x, dx)) * 4 + zxor(j)) * 64
        size = 64
        if part is not None:
            off, size = off + 32 * part, 32
        return wbuf.at[pl.ds(pl.multiple_of(off, size), size)]

    def step(j, first, d):
        along_x = (j % 2 == 0) == first
        return at_x(d) if along_x else at_y(d)

    def source(j, a):
        return w_ref if j == 0 and a == 0 else chunk(j, a, 0)

    def second(j, a):
        src = source(j, a)
        send(("u1", j, a), src, chunk(j, a, 0), step(j, False, 1))
        send(("u2", j, a), src, chunk(j, a, 0), step(j, False, -1))

    def s1(j):
        src = source(j, 0)
        send(("t1", j), src, chunk(j, 0, 0), step(j, True, 1))
        send(("t2", j), src, chunk(j, 0, 0), step(j, True, -1))
        second(j, 0)

    def s2_(j):
        recv(("t1", j), chunk(j, -1, 0), step(j, True, 1))
        send(("t3", j), chunk(j, -1, 0, 0), chunk(j, -1, 0, 0), step(j, True, 1))
        recv(("t2", j), chunk(j, 1, 0), step(j, True, -1))
        send(("t4", j), chunk(j, 1, 0, 1), chunk(j, 1, 0, 1), step(j, True, -1))
        second(j, -1)
        second(j, 1)

    def s3_(j):
        recv(("t3", j), chunk(j, 2, 0, 0), step(j, True, 1))
        recv(("t4", j), chunk(j, 2, 0, 1), step(j, True, -1))
        second(j, 2)

    def relay(j, a):
        recv(("u1", j, a), chunk(j, a, -1), step(j, False, 1))
        send(("u3", j, a), chunk(j, a, -1, 0), chunk(j, a, -1, 0), step(j, False, 1))
        recv(("u2", j, a), chunk(j, a, 1), step(j, False, -1))
        send(("u4", j, a), chunk(j, a, 1, 1), chunk(j, a, 1, 1), step(j, False, -1))

    def last(j, a):
        recv(("u3", j, a), chunk(j, a, 2, 0), step(j, False, 1))
        recv(("u4", j, a), chunk(j, a, 2, 1), step(j, False, -1))

    def own_place(j):
        return wbuf.at[pl.ds(pl.multiple_of(((y * 4 + x) * 4 + zxor(j)) * 64, 64), 64)]

    def half_of(p):
        return zl // 2 if p == 0 else 1 - zl // 2

    t_sib, t_acr, t_dia = zh * 2 + 1 - c, (1 - zh) * 2 + c, (1 - zh) * 2 + 1 - c
    to_sum = make("k2b", ggs.at[t_dia, half_of(1)], x0.at[1], sibling)
    to_sibling = make("k1b", ggs.at[t_sib, half_of(1)], gs0.at[1], sibling)
    to_far = make("k3b", xs.at[1], ga0.at[1], across)

    def batch(p, dy):
        yy, h = shift(y, dy), half_of(p)

        def one(i, carry):
            rows = pl.ds(pl.multiple_of(yy * 1024 + i * 256 + h * 128, 128), 128)
            part = dot(cot_ref[...], wbuf[rows, :], ((1,), (1,)))
            ggs[yy, h, i] = part.astype(BF16)
            return carry

        lax.fori_loop(0, 4, one, 0, unroll=True)
        if p == 1:

            @pl.when(yy == t_dia)
            def _():
                to_sum.start()

            @pl.when(yy == t_sib)
            def _():
                to_sibling.start()

    def far_share(dy):
        @pl.when(shift(y, dy) == t_acr)
        def _():
            to_sum.wait_recv()
            xs[1] = (ggs[t_acr, half_of(1)].astype(F32) + x0[1].astype(F32)).astype(BF16)
            to_far.start()

    gg_base = 160
    halo_base = 168

    row = lax.broadcasted_iota(jnp.int32, (2 * LEN, 128), 0)
    sign = (1 - 2 * lax.rem(row, 2)).astype(F32)
    inner = lax.broadcasted_iota(jnp.int32, (LEN, 128), 0) != 0

    def dft(val):
        return dot(fa_ref[0], val) + dot(fa_ref[1], val)

    def idft(val):
        hi = val.astype(BF16)
        lo = (val - hi.astype(F32)).astype(BF16)
        return dot(ia_ref[0], hi) + dot(ia_ref[0], lo) + dot(ia_ref[1], hi)

    def cmul(a, b, conj):
        ar, ai, br, bi = a[:LEN], a[LEN:], b[:LEN], b[LEN:]
        ii = ai * bi
        if conj:
            re = ar * br + jnp.where(inner, ii, 0.0)
            im = jnp.where(inner, ai * br - ar * bi, ii)
        else:
            re = ar * br - jnp.where(inner, ii, 0.0)
            im = jnp.where(inner, ai * br + ar * bi, ii)
        return jnp.concatenate([re, im], 0)

    def strips(fn):
        def one(e, carry):
            fn(e, pl.ds(pl.multiple_of(e * 128, 128), 128))
            return carry

        lax.fori_loop(0, 8, one, 0, unroll=True)

    here = seg_ref[s]
    back = seg_ref[jnp.maximum(s - 1, 0)]
    ahead = seg_ref[jnp.minimum(s + 1, 63)]
    linked = jnp.where(jnp.logical_and(s > 0, here == back), 1.0, 0.0).astype(F32)
    linked_next = jnp.where(jnp.logical_and(s < 63, here == ahead), 1.0, 0.0).astype(F32)

    def rows_of(place, size):
        return pl.ds(pl.multiple_of(place * size, size), size)

    def half_copy(base, h, src, dst, dev):
        return pltpu.make_async_remote_copy(
            src_ref=src,
            dst_ref=dst,
            send_sem=ss.at[base + h],
            recv_sem=rs.at[base + h],
            device_id=dev,
            device_id_type=MESH,
        )

    def half_tail(p):
        h = half_of(p)
        if p == 0:
            recv("k1", gs0.at[0], sibling)
            recv("k3", ga0.at[0], across)
        else:
            to_sibling.wait_recv()
            to_far.wait_recv()

        def cols_of(i):
            return pl.ds(pl.multiple_of(i * 256 + h * 128, 128), 128)

        def gradients(i, carry):
            cols = cols_of(i)
            total = ggs[t, h, i].astype(F32)
            total = total + gs0[p, i].astype(F32) + ga0[p, i].astype(F32)
            gg = total.astype(BF16).astype(F32)
            gfb[h, i] = (gg * q_ref[:, cols].astype(F32)).astype(BF16)
            gq_ref[:, cols] = (gg * fil[:, cols].astype(F32)).astype(BF16)
            return carry

        lax.fori_loop(0, 4, gradients, 0, unroll=True)
        half_copy(halo_base, h, gfb.at[h], gnx.at[h], at_s(-1)).start()

        def taps_part(i, carry):
            cols = cols_of(i)
            spec = dft(gfb[h, i])
            e = i * 2 + h
            gft[e] = spec
            part = idft(cmul(spec, xbuf[e], True)).T
            tgf[cols, :] = part
            tgs[cols, :] = part.astype(BF16)
            return carry

        lax.fori_loop(0, 4, taps_part, 0, unroll=True)
        for d in (2, 1, 3):
            rows = pl.ds(pl.multiple_of(shift(y, d) * 256 + h * 128, 128), 128)
            here = pl.ds(pl.multiple_of(h * 128, 128), 128)
            send(("r1", p, d), tgs.at[rows], r1.at[d - 1, here], at_y(d))

    def r1_rows(p):
        return pl.ds(pl.multiple_of(half_of(p) * 128, 128), 128)

    def backward(h):
        half_copy(halo_base, h, gfb.at[h], gnx.at[h], at_s(-1)).wait_recv()

        def one(i, carry):
            e = i * 2 + h
            cols = pl.ds(pl.multiple_of(e * 128, 128), 128)
            spec = gft[e] + linked_next * (sign * dft(gnx[h, i]))
            gp = idft(cmul(spec, tbuf[e], True)).astype(BF16).astype(F32)
            gk_ref[:, cols] = (gp * v_ref[:, cols].astype(F32)).astype(BF16)
            gv_ref[:, cols] = (gp * k_ref[:, cols].astype(F32)).astype(BF16)
            return carry

        lax.fori_loop(0, 4, one, 0, unroll=True)

    for cp in loads[3:]:
        cp.wait()
    pl.semaphore_wait(barrier, len(partners))

    s1(0)
    send("z1", w_ref, own_place(0), at_z(1))
    send("z2", w_ref, own_place(0), at_z(2))
    send("halo", prod, prev, at_s(1))

    def spectra(e, cols):
        tap = taps_ref[cols, :]
        tbuf[e] = dot(fa_ref[0], tap, ((1,), (1,))) + dot(fa_ref[1], tap, ((1,), (1,)))
        xbuf[e] = dft(prod[:, cols])

    strips(spectra)
    own_w.wait()

    recv("z1", own_place(1), at_z(1))
    send("z3", own_place(1), own_place(1), at_z(2))
    s1(1)
    s2_(0)
    s2_(1)
    s3_(0)
    s3_(1)
    relay(0, 0)
    relay(1, 0)
    recv("z2", own_place(2), at_z(2))
    s1(2)
    recv("halo", prev, at_s(1))

    def forward(e, cols):
        spec = xbuf[e] + linked * (sign * dft(prev[:, cols]))
        xbuf[e] = spec
        filt = idft(cmul(spec, tbuf[e], False)).astype(BF16)
        fil[:, cols] = filt
        gbuf[t, :, cols] = (q_ref[:, cols].astype(F32) * filt.astype(F32)).astype(BF16)

    strips(forward)
    send("g2", gbuf.at[t], gbuf.at[t], across)
    send("g1", gbuf.at[t], gbuf.at[t], sibling)

    relay(0, -1)
    relay(1, -1)
    relay(0, 1)
    relay(1, 1)
    recv("z3", own_place(3), at_z(2))
    s1(3)
    s2_(2)
    relay(0, 2)
    relay(1, 2)
    s2_(3)
    last(0, 0)
    last(1, 0)
    batch(0, 0)
    s3_(2)
    s3_(3)
    relay(2, 0)
    relay(3, 0)
    for a in (-1, 1):
        last(0, a)
        last(1, a)
    last(0, 2)
    batch(0, -1)
    relay(2, -1)
    relay(3, -1)
    batch(0, 1)
    relay(2, 1)
    relay(3, 1)
    last(1, 2)
    batch(0, 2)
    first = half_of(0)
    send("k2", ggs.at[t_dia, first], x0.at[0], sibling)
    send("k1", ggs.at[t_sib, first], gs0.at[0], sibling)
    relay(2, 2)
    relay(3, 2)
    recv("k2", x0.at[0], sibling)
    xs[0] = (ggs[t_acr, first].astype(F32) + x0[0].astype(F32)).astype(BF16)
    send("k3", xs.at[0], ga0.at[0], across)
    last(2, 0)
    last(3, 0)
    batch(1, 0)
    for a in (-1, 1):
        last(2, a)
        last(3, a)
    last(2, 2)
    batch(1, -1)
    far_share(0)
    batch(1, 1)
    far_share(-1)
    last(3, 2)
    far_share(1)
    batch(1, 2)
    far_share(2)

    half_tail(0)
    recv("g2", gbuf.at[t_acr], across)
    send("g3", gbuf.at[t_acr], gbuf.at[t_acr], sibling)
    half_tail(1)

    @pl.when(lax.rem(zl, 2) == 0)
    def _():
        backward(half_of(0))

    def outputs(n):
        cols = pl.ds(n * 256, 256)
        total = dot(gbuf[0], wbuf[0:1024, cols])
        for i in range(1, 4):
            total = total + dot(gbuf[i], wbuf[i * 1024 : (i + 1) * 1024, cols])
        out_ref[:, cols] = total.astype(BF16)

    for p in range(2):
        for d in range(1, 4):
            recv(("r1", p, d), r1.at[d - 1, r1_rows(p)], at_y(d))
    total = tgf[rows_of(y, 256), :]
    for d in range(3):
        total = total + r1[d].astype(F32)
    s2[...] = total
    for d in (2, 1, 3, 0):
        for j in (3, 2, 1, 0):
            if d or j:
                rows = rows_of(shift(x, d) * 4 + zxor(j), 16)
                send(("r2", d, j), s2.at[rows], r2.at[d * 4 + j], at_xz(d, j))

    recv("g1", gbuf.at[t_sib], sibling)
    recv("g3", gbuf.at[t_dia], sibling)
    for n in range(4):
        outputs(n)
    backward(half_of(1))

    @pl.when(lax.rem(zl, 2) == 1)
    def _():
        backward(half_of(0))

    total = s2[rows_of(x * 4 + zl, 16), :]
    for d in range(4):
        for j in range(4):
            if d or j:
                recv(("r2", d, j), r2.at[d * 4 + j], at_xz(d, j))
                total = total + r2[d * 4 + j]
    tg_ref[...] = total

    for h in range(2):
        half_copy(halo_base, h, gfb.at[h], gnx.at[h], at_s(-1)).wait_send()
    for cp in sends:
        cp.wait_send()
    for cp in (to_sum, to_sibling, to_far):
        cp.wait_send()

    assert len(keys_of) <= gg_base


def write_out(*refs):
    ins, outs, bufs, sem = refs[:5], refs[5:10], refs[10:15], refs[15]
    reads = [pltpu.make_async_copy(ins[i], bufs[i], sem.at[i]) for i in range(5)]
    writes = [pltpu.make_async_copy(bufs[i], outs[i], sem.at[5 + i]) for i in range(5)]
    for cp in reads:
        cp.start()
    for read, write in zip(reads, writes):
        read.wait()
        write.start()
    for cp in writes:
        cp.wait()


def on_device(queries, keys, values, w_out, taps, seg_ids, cotangent):
    fwd, inv = dft_tables()
    block = queries.shape
    vmem = pl.BlockSpec(memory_space=pltpu.VMEM)
    hbm = pl.BlockSpec(memory_space=pl.ANY)
    smem = pl.BlockSpec(memory_space=pltpu.SMEM)
    outs = [jax.ShapeDtypeStruct(block, BF16)] * 4 + [jax.ShapeDtypeStruct((16, LEN), F32)]
    scratch = [
        pltpu.VMEM(block, BF16),
        pltpu.VMEM(block, BF16),
        pltpu.VMEM(block, BF16),
        pltpu.VMEM((64, 1024), BF16),
        pltpu.VMEM((1024, LEN), BF16),
        pltpu.VMEM(block, BF16),
        pltpu.VMEM((2, 256, 128), BF16),
        pltpu.VMEM((2, 128, 256), BF16),
        pltpu.VMEM((4096, 1024), BF16),
        pltpu.VMEM(block, BF16),
        pltpu.VMEM(block, BF16),
        pltpu.VMEM((8, 256, 128), F32),
        pltpu.VMEM((8, 256, 128), F32),
        pltpu.VMEM(block, BF16),
        pltpu.VMEM((4, *block), BF16),
        pltpu.VMEM((4, 2, 4, 128, 128), BF16),
        pltpu.VMEM((2, 4, 128, 128), BF16),
        pltpu.VMEM((2, 4, 128, 128), BF16),
        pltpu.VMEM((2, 4, 128, 128), BF16),
        pltpu.VMEM((2, 4, 128, 128), BF16),
        pltpu.VMEM((2, 4, 128, 128), BF16),
        pltpu.VMEM((2, 4, 128, 128), BF16),
        pltpu.VMEM((8, 256, 128), F32),
        pltpu.VMEM((1024, LEN), F32),
        pltpu.VMEM((1024, LEN), BF16),
        pltpu.VMEM((3, 256, LEN), BF16),
        pltpu.VMEM((256, LEN), F32),
        pltpu.VMEM((16, 16, LEN), F32),
        pltpu.SemaphoreType.DMA((170,)),
        pltpu.SemaphoreType.DMA((170,)),
        pltpu.SemaphoreType.DMA((9,)),
    ]
    results = pl.pallas_call(
        kernel,
        out_shape=outs,
        in_specs=[hbm] * 5 + [smem] + [hbm] * 3,
        out_specs=[vmem] * 5,
        scratch_shapes=scratch,
        compiler_params=pltpu.CompilerParams(
            collective_id=0, has_side_effects=True, vmem_limit_bytes=67043328
        ),
        name="hyena",
    )(queries, keys, values, w_out, taps, seg_ids, cotangent, jnp.asarray(fwd), jnp.asarray(inv))
    return pl.pallas_call(
        write_out,
        out_shape=outs,
        in_specs=[hbm] * 5,
        out_specs=[hbm] * 5,
        scratch_shapes=[pltpu.VMEM(o.shape, o.dtype) for o in outs]
        + [pltpu.SemaphoreType.DMA((10,))],
        compiler_params=pltpu.CompilerParams(vmem_limit_bytes=67043328),
        name="write_out",
    )(*results)


def solution(mesh):
    split = Mesh(mesh.devices.reshape(4, 4, 4, 2, 2), AXES)
    rows = P(SEQ, TP)
    in_specs = (rows, rows, rows, rows, P(TP, None), P(), rows)
    out_specs = (rows, rows, rows, rows, P(TP + SEQ, None))
    return jax.shard_map(
        on_device, mesh=split, in_specs=in_specs, out_specs=out_specs, check_vma=False
    )
```
